256 devices in a mesh: head: 4 (over y), seq: 64 (over x, z, core).
Axes of the slice: x: 4, y: 4, z: 8, core: 2. Of those that a mesh axis runs over, the one named last changes fastest.
Arguments:
- queries: bfloat16 [8, 16, 32, 128], P(None, None, 'head'), may hold values from -4000 to 4000
- cache_keys: bfloat16 [16, 16, 8192, 128], P(None, 'head', 'seq'), may hold values from -6 to 6
- stored_values: bfloat16 [16, 16, 8192, 128], P(None, 'head', 'seq'), may hold values from -6 to 6
- new_keys: bfloat16 [8, 16, 16, 128], P(None, None, 'head'), may hold values from -12 to 12
- decoded_values: bfloat16 [8, 16, 16, 128], P(None, None, 'head'), may hold values from -6 to 6
- keep_mask: int32 [16, 8192], P(None, 'seq'), may hold values from 0 to 1
Outputs:
- attended: bfloat16 [8, 16, 4096], P(None, None, 'head')
- importance: float32 [16, 8192], P('head', 'seq')
The draws below stay inside these ranges and needn't reach their ends.
All inputs are finite; a program needn't handle non-finite values.
Results may differ from the reference program's by a relative error of at most 0.0034.
Values sent between devices are 32-bit elements; how exact they have to be, the bound alone decides.
A program may use at most 128 MiB of HBM per device.

```python
import jax
import jax.numpy as jnp
from jax import lax

HQ = 32
KEY_VALUE_HEADS = 16
HEAD_SIZE = 128
BATCH_SEQUENCES = 16
BLOCK_TOKENS = 128
DECODE_STEPS = 8
CONTEXT_TOKENS = 8192


def base_queries(key):
    return jax.random.truncated_normal(jax.random.fold_in(key, 31), -6.0, 6.0, (DECODE_STEPS, BATCH_SEQUENCES, HQ, HEAD_SIZE), jnp.float32)


def chosen_positions(key):
    first_pos = jax.random.randint(jax.random.fold_in(key, 51), (BATCH_SEQUENCES,), 0, CONTEXT_TOKENS)
    second_pos = (first_pos + CONTEXT_TOKENS // 2) % CONTEXT_TOKENS
    return (first_pos, second_pos)


def drawn_keys(key):
    key_rows = jax.random.truncated_normal(jax.random.fold_in(key, 41), -6.0, 6.0, (BATCH_SEQUENCES, KEY_VALUE_HEADS, CONTEXT_TOKENS, HEAD_SIZE), jnp.float32)
    return key_rows


def draw_cache_keys(key, part):
    key_rows = drawn_keys(key)
    return key_rows.astype(jnp.bfloat16)


def draw_queries(key, part):
    query_rows = base_queries(key)
    return query_rows.astype(jnp.bfloat16)


def draw_new_keys(key, part):
    query_rows = base_queries(key)
    paired = query_rows[:, :, 0::2, :] + query_rows[:, :, 1::2, :]
    random_jitter = jax.random.truncated_normal(jax.random.fold_in(key, 71), -6.0, 6.0, (DECODE_STEPS, BATCH_SEQUENCES, KEY_VALUE_HEADS, HEAD_SIZE), jnp.float32)
    return (0.7 * paired + 0.5 * random_jitter).astype(jnp.bfloat16)


def draw_keep_mask(key, part):
    kept = jax.random.randint(jax.random.fold_in(key, 81), (BATCH_SEQUENCES, CONTEXT_TOKENS), 0, 4) > 0
    first_pos, second_pos = chosen_positions(key)
    places = jnp.arange(CONTEXT_TOKENS)[None, :]
    forced = (places == first_pos[:, None]) | (places == second_pos[:, None])
    return (kept | forced).astype(jnp.int32)


def steps_of(own_key, extent, split, low, largest):
    factor_of, own = 1.0, jax.random.fold_in(own_key, 6)
    for position, parts in split:
        draws = jnp.exp(jax.random.uniform(jax.random.fold_in(own, position), (parts,), jnp.float32, low / len(split), largest / len(split)))
        factor_of = factor_of * jnp.repeat(draws, extent[position] // parts).reshape([-1 if axis == position else 1 for axis in range(len(extent))])
    return factor_of


def bell_draw(key, extent, width, most, split=(), dtype=jnp.bfloat16):
    array = jax.random.normal(key, extent, jnp.float32) * width
    if len(split) > 0:
        array = steps_of(key, extent, split, -0.22, 0.18) * array
    return jnp.clip(array, min=-most, max=most).astype(dtype)


def setup_inputs(seed: int = 0) -> dict:
    streams_of = jax.random.split(jax.random.key(seed), 7)
    return {
        "queries": draw_queries(jax.random.fold_in(streams_of[6], 71), 0),
        "cache_keys": draw_cache_keys(jax.random.fold_in(streams_of[6], 71), 0),
        "stored_values": bell_draw(streams_of[2], (BATCH_SEQUENCES, KEY_VALUE_HEADS, CONTEXT_TOKENS, HEAD_SIZE), 1.0, 6.0, ((1, 4), (2, 64))),
        "new_keys": draw_new_keys(jax.random.fold_in(streams_of[6], 71), 0),
        "decoded_values": bell_draw(streams_of[4], (DECODE_STEPS, BATCH_SEQUENCES, KEY_VALUE_HEADS, HEAD_SIZE), 1.0, 6.0, ((2, 4),)),
        "keep_mask": draw_keep_mask(jax.random.fold_in(streams_of[6], 71), 0),
    }


score_scale = 1.0 / 12.0
far_below = -1e30


def one_row(inputs):
    query_rows, key_cache, value_store_cache, fresh_keys, fresh_values, kept_row = inputs
    block_count = CONTEXT_TOKENS // BLOCK_TOKENS
    grouped_queries = query_rows.astype(jnp.float32).reshape(DECODE_STEPS, KEY_VALUE_HEADS, 2, HEAD_SIZE)
    logit_scores = jnp.einsum('thgd,hsd->thgs', grouped_queries, key_cache.astype(jnp.float32)) * score_scale
    scores_per_block = logit_scores.reshape(DECODE_STEPS, KEY_VALUE_HEADS, 2, block_count, BLOCK_TOKENS)
    block_keep = (kept_row > 0).reshape(block_count, BLOCK_TOKENS)
    block_peak = jnp.max(jnp.where(block_keep, scores_per_block, far_below), axis=-1)
    block_exp = jnp.where(block_keep, jnp.exp(scores_per_block - block_peak[..., None]), 0.0)
    block_total = jnp.sum(block_exp, axis=-1)
    block_weights = lax.optimization_barrier(block_exp.astype(jnp.bfloat16)).astype(jnp.float32)
    blocked_values = value_store_cache.astype(jnp.float32).reshape(KEY_VALUE_HEADS, block_count, BLOCK_TOKENS, HEAD_SIZE)
    block_sum = jnp.einsum('thgks,hksd->thgkd', block_weights, blocked_values)
    new_scores = jnp.einsum('thgd,jhd->thgj', grouped_queries, fresh_keys.astype(jnp.float32)) * score_scale
    causal = (jnp.arange(DECODE_STEPS)[None, :] <= jnp.arange(DECODE_STEPS)[:, None])[:, None, None, :]
    new_peak = jnp.max(jnp.where(causal, new_scores, far_below), axis=-1)
    new_exp = jnp.where(causal, jnp.exp(new_scores - new_peak[..., None]), 0.0)
    new_total = jnp.sum(new_exp, axis=-1)
    new_weights = lax.optimization_barrier(new_exp.astype(jnp.bfloat16)).astype(jnp.float32)
    new_sum = jnp.einsum('thgj,jhd->thgd', new_weights, fresh_values.astype(jnp.float32))
    peak = jnp.maximum(jnp.max(block_peak, axis=-1), new_peak)
    block_factor = jnp.exp(block_peak - peak[..., None])
    new_factor = jnp.exp(new_peak - peak)
    total = jnp.sum(block_total * block_factor, axis=-1) + new_total * new_factor
    weighted = jnp.sum(block_sum * block_factor[..., None], axis=3) + new_sum * new_factor[..., None]
    attended = (weighted / total[..., None]).astype(jnp.bfloat16).reshape(DECODE_STEPS, HQ * HEAD_SIZE)
    kept = (kept_row > 0)[None, None, None, :]
    shares = jnp.where(kept, jnp.exp(logit_scores - peak[..., None]), 0.0) / total[..., None]
    importance = jnp.sum(shares, axis=(0, 1, 2)) * (CONTEXT_TOKENS / (DECODE_STEPS * HQ))
    return attended, importance


def reference(queries, cache_keys, stored_values, new_keys, decoded_values, keep_mask):
    inputs = (jnp.swapaxes(queries, 0, 1), cache_keys, stored_values,
              jnp.swapaxes(new_keys, 0, 1), jnp.swapaxes(decoded_values, 0, 1), keep_mask)
    attended, importance = lax.map(one_row, inputs)
    return jnp.swapaxes(attended, 0, 1), importance
```

```python
import jax
import jax.numpy as jnp
from jax import lax
from jax.experimental import pallas as pl
from jax.experimental.pallas import tpu as pltpu
from jax.sharding import Mesh
from jax.sharding import PartitionSpec as P

F32 = jnp.float32
BF16 = jnp.bfloat16
MESH = pl.DeviceIdType.MESH
SCALE = 1.0 / 12.0
FAR_BELOW = -1e30

T, B, H, D = 8, 16, 8, 128
KV = 4
S = 128
NY, NX, NZ, NC = 4, 4, 8, 2
FAR_FIRST = (4, 3, 5, 2, 6, 1, 7)
HEADS_ALL = 32
CONTEXT = S * NX * NZ * NC


def lane_of(tile, lane):
    return jnp.broadcast_to(tile[:, lane : lane + 1], (H, D))


def to_front(tile, lane):
    return pltpu.roll(tile, lax.rem(128 - lane, 128), 1)


def expand_heads(rows):
    sub = lax.broadcasted_iota(jnp.int32, (H, D), 0)
    out = jnp.broadcast_to(rows[KV - 1 : KV], (H, D))
    for k in range(KV - 2, -1, -1):
        out = jnp.where(sub < 2 * (k + 1), jnp.broadcast_to(rows[k : k + 1], (H, D)), out)
    return out


def kernel(
    q_hbm, k_hbm, v_hbm, nk_hbm, nv_hbm, mask_hbm,
    out_ref, imp_ref,
    q_ref, k_ref, v_ref, nk_ref, nv_ref, mask_ref,
    sums, exps, peaks, core_in, pair, x_in, x_sum, z_in, gathered, imp_part, imp_in,
    stat_own, stat_core, stat_pair, stat_x, stat_group, stat_z,
    in_sem, kv_sem,
    cs_s, cs_r, cd_s, cd_r, xs_s, xs_r, xd_s, xd_r, zs_s, zs_r, zd_s, zd_r, y_s, y_r,
    gz_s, gz_r, gx_s, gx_r, gc_s, gc_r,
):
    my = lax.axis_index("head")
    mx = lax.axis_index("seq_0")
    mz = lax.axis_index("seq_1")
    mc = lax.axis_index("seq_2")
    other = 1 - mc
    t_own = NX * mc + mx
    b_own = 2 * mz

    def core_dev():
        return {"seq_2": other}

    def x_dev(d):
        return {"seq_0": lax.rem(mx + d, NX)}

    def z_dev(d):
        return {"seq_1": lax.rem(mz + d, NZ)}

    def y_dev(d):
        return {"head": lax.rem(my + d, NY)}

    def remote(src, dst, ss, rs, dev):
        return pltpu.make_async_remote_copy(
            src_ref=src, dst_ref=dst, send_sem=ss, recv_sem=rs, device_id=dev, device_id_type=MESH
        )

    barrier = pltpu.get_barrier_semaphore()
    partners = (
        [core_dev()]
        + [x_dev(d) for d in range(1, NX)]
        + [z_dev(d) for d in FAR_FIRST]
        + [y_dev(d) for d in range(1, NY)]
    )
    for dev in partners:
        pl.semaphore_signal(barrier, inc=1, device_id=dev, device_id_type=MESH)

    small = [
        pltpu.make_async_copy(q_hbm, q_ref, in_sem.at[0]),
        pltpu.make_async_copy(mask_hbm, mask_ref, in_sem.at[1]),
        pltpu.make_async_copy(nk_hbm.at[:, pl.ds(b_own, 2)], nk_ref, in_sem.at[2]),
        pltpu.make_async_copy(nv_hbm.at[:, pl.ds(b_own, 2)], nv_ref, in_sem.at[3]),
    ]
    for copy in small:
        copy.start()

    def k_copy(b):
        return pltpu.make_async_copy(k_hbm.at[b], k_ref.at[b], kv_sem.at[0, b])

    def v_copy(b):
        return pltpu.make_async_copy(v_hbm.at[b], v_ref.at[b], kv_sem.at[1, b])

    def start_loads(b, _):
        k_copy(b).start()
        v_copy(b).start()
        return 0

    lax.fori_loop(0, B, start_loads, 0)
    for copy in small:
        copy.wait()

    lane = lax.broadcasted_iota(jnp.int32, (H, D), 1)
    sub = lax.broadcasted_iota(jnp.int32, (H, D), 0)
    row_kv = lax.rem(lax.broadcasted_iota(jnp.int32, (T * H, S), 0), H) // 2

    def one_row(b, carry):
        peak_tile, total_tile = carry
        k_copy(b).wait()
        v_copy(b).wait()
        q = q_ref[:, b].astype(F32).reshape(T * H, D).astype(BF16)
        scores = lax.dot_general(
            q, k_ref[b].reshape(KV * S, D), (((1,), (1,)), ((), ())), preferred_element_type=F32
        )
        s = scores[:, (KV - 1) * S :]
        for k in range(KV - 2, -1, -1):
            s = jnp.where(row_kv == k, scores[:, k * S : (k + 1) * S], s)
        s = s * SCALE
        keep = jnp.broadcast_to(mask_ref[pl.ds(b, 1), :], (T * H, S)) > 0
        m = jnp.max(jnp.where(keep, s, FAR_BELOW), axis=1, keepdims=True)
        e = jnp.where(keep, jnp.exp(s - m), 0.0)
        total = jnp.sum(e, axis=1, keepdims=True)
        exps[b] = e.reshape(T, H, S)
        weights = jnp.concatenate(
            [jnp.where(row_kv == k, e, 0.0).astype(BF16) for k in range(KV)], axis=1
        )
        o = jnp.dot(weights, v_ref[b].reshape(KV * S, D), preferred_element_type=F32)
        sums[b] = o.reshape(T, H, D)
        for t in range(T):
            here = lane == t * B + b
            peak_tile = jnp.where(here, jnp.broadcast_to(m[t * H : (t + 1) * H], (H, D)), peak_tile)
            total_tile = jnp.where(
                here, jnp.broadcast_to(total[t * H : (t + 1) * H], (H, D)), total_tile
            )
        return peak_tile, total_tile

    zero = jnp.zeros((H, D), F32)
    block_peak, block_total = lax.fori_loop(0, B, one_row, (zero, zero))
    peaks[...] = block_peak

    peak_tile, total_tile = block_peak, block_total
    for i in range(2):
        b = b_own + i
        here = lane == t_own * B + b
        q = q_ref[t_own, b].astype(F32)
        ns = []
        for j in range(T):
            prod = q * expand_heads(nk_ref[j, i].astype(F32))
            sj = jnp.broadcast_to(jnp.sum(prod, axis=1, keepdims=True), (H, D)) * SCALE
            ns.append(jnp.where(j <= t_own, sj, FAR_BELOW))
        new_peak = ns[0]
        for j in range(1, T):
            new_peak = jnp.maximum(new_peak, ns[j])
        new_total, new_sum = zero, zero
        for j in range(T):
            ej = jnp.where(j <= t_own, jnp.exp(ns[j] - new_peak), 0.0)
            new_total = new_total + ej
            new_sum = new_sum + ej.astype(BF16).astype(F32) * expand_heads(nv_ref[j, i].astype(F32))
        old_peak = jnp.max(jnp.where(here, block_peak, -3e38), axis=1, keepdims=True)
        old_total = jnp.sum(jnp.where(here, block_total, 0.0), axis=1, keepdims=True)
        old_peak = jnp.broadcast_to(old_peak, (H, D))
        old_total = jnp.broadcast_to(old_total, (H, D))
        both = jnp.maximum(old_peak, new_peak)
        f_old = jnp.exp(old_peak - both)
        f_new = jnp.exp(new_peak - both)
        sums[b, t_own] = sums[b, t_own] * f_old + new_sum * f_new
        peak_tile = jnp.where(here, both, peak_tile)
        total_tile = jnp.where(here, old_total * f_old + new_total * f_new, total_tile)
    stat_own[0] = peak_tile
    stat_own[1] = total_tile

    pl.semaphore_wait(barrier, len(partners))

    order = [lax.rem(mz + d, NZ) for d in FAR_FIRST] + [mz]
    core_stat = remote(stat_own, stat_core, cs_s, cs_r, core_dev())
    core_stat.start()
    core_copies = []
    for k, zz in enumerate(order):
        copy = remote(
            sums.at[pl.ds(2 * zz, 2), pl.ds(NX * other, NX)],
            core_in.at[k],
            cd_s.at[k],
            cd_r.at[k],
            core_dev(),
        )
        copy.start()
        core_copies.append(copy)
    core_stat.wait_recv()
    peak_c, total_c = stat_core[0], stat_core[1]
    pair_peak = jnp.maximum(peak_tile, peak_c)
    f_own = jnp.exp(peak_tile - pair_peak)
    f_core = jnp.exp(peak_c - pair_peak)
    pair_total = total_tile * f_own + total_c * f_core
    stat_pair[0] = pair_peak
    stat_pair[1] = pair_total

    x_stats = []
    for d in range(1, NX):
        copy = remote(stat_pair, stat_x.at[d - 1], xs_s.at[d - 1], xs_r.at[d - 1], x_dev(d))
        copy.start()
        x_stats.append(copy)
    x_copies = []
    for k, zz in enumerate(order):
        core_copies[k].wait_recv()
        fo = to_front(f_own, NX * mc * B + 2 * zz)
        fc = to_front(f_core, NX * mc * B + 2 * zz)
        for tl in range(NX):
            for i in range(2):
                at = tl * B + i
                pair[k, tl, i] = (
                    sums[2 * zz + i, NX * mc + tl] * lane_of(fo, at)
                    + core_in[k, i, tl] * lane_of(fc, at)
                )
        row = []
        for d in (2, 1, 3):
            copy = remote(
                pair.at[k, lax.rem(mx + d, NX)],
                x_in.at[k, d - 1],
                xd_s.at[k, d - 1],
                xd_r.at[k, d - 1],
                x_dev(d),
            )
            copy.start()
            row.append(copy)
        x_copies.append(row)
    for copy in x_stats:
        copy.wait_recv()
    group_peak = pair_peak
    for d in range(1, NX):
        group_peak = jnp.maximum(group_peak, stat_x[d - 1, 0])
    f_mine = jnp.exp(pair_peak - group_peak)
    group_total = pair_total * f_mine
    f_peer = []
    for d in range(1, NX):
        f = jnp.exp(stat_x[d - 1, 0] - group_peak)
        f_peer.append(f)
        group_total = group_total + stat_x[d - 1, 1] * f
    stat_group[0] = group_peak
    stat_group[1] = group_total

    z_stats = []
    for d in FAR_FIRST:
        copy = remote(stat_group, stat_z.at[d - 1], zs_s.at[d - 1], zs_r.at[d - 1], z_dev(d))
        copy.start()
        z_stats.append(copy)
    z_copies = []
    for k, zz in enumerate(order):
        for copy in x_copies[k]:
            copy.wait_recv()
        front = t_own * B + 2 * zz
        fm = to_front(f_mine, front)
        fp = [to_front(f, front) for f in f_peer]
        for i in range(2):
            acc = pair[k, mx, i] * lane_of(fm, i)
            for d in range(1, NX):
                acc = acc + x_in[k, d - 1, i] * lane_of(fp[d - 1], i)
            x_sum[k, i] = acc
        if k < NZ - 1:
            d = FAR_FIRST[k]
            copy = remote(x_sum.at[k], z_in.at[d - 1], zd_s.at[d - 1], zd_r.at[d - 1], z_dev(d))
            copy.start()
            z_copies.append(copy)
    for copy in z_stats:
        copy.wait_recv()
    peak = group_peak
    for d in range(1, NZ):
        peak = jnp.maximum(peak, stat_z[d - 1, 0])
    f_mine = jnp.exp(group_peak - peak)
    total = group_total * f_mine
    f_peer = []
    for d in range(1, NZ):
        f = jnp.exp(stat_z[d - 1, 0] - peak)
        f_peer.append(f)
        total = total + stat_z[d - 1, 1] * f
    inverse = 1.0 / total
    front = t_own * B + b_own
    fm = to_front(f_mine * inverse, front)
    fp = [to_front(f * inverse, front) for f in f_peer]
    for copy in z_copies:
        copy.wait_recv()
    for i in range(2):
        acc = x_sum[NZ - 1, i] * lane_of(fm, i)
        for d in range(1, NZ):
            acc = acc + z_in[d - 1, i] * lane_of(fp[d - 1], i)
        gathered[t_own, b_own + i] = acc

    def piece(t, zz):
        return gathered.at[t, pl.ds(2 * zz, 2)]

    gz = {}
    for d in FAR_FIRST:
        copy = remote(piece(t_own, mz), piece(t_own, mz), gz_s.at[d - 1], gz_r.at[d - 1], z_dev(d))
        copy.start()
        gz[d] = copy
    gx, gc = {}, {}

    def forward_x(d):
        zz = lax.rem(mz + NZ - d, NZ)
        for dx in (2, 1, 3):
            copy = remote(
                piece(t_own, zz), piece(t_own, zz), gx_s.at[d, dx - 1], gx_r.at[d, dx - 1], x_dev(dx)
            )
            copy.start()
            gx[d, dx] = copy

    def forward_core(d, dx):
        zz = lax.rem(mz + NZ - d, NZ)
        t = NX * mc + lax.rem(mx + NX - dx, NX)
        copy = remote(piece(t, zz), piece(t, zz), gc_s.at[d, dx], gc_r.at[d, dx], core_dev())
        copy.start()
        gc[d, dx] = copy

    forward_x(0)
    forward_core(0, 0)

    share = jnp.exp(peaks[...] - peak) * inverse * (CONTEXT / (DECODE * HEADS_ALL))
    for b in range(B):
        acc = exps[b, 0] * lane_of(share, b)
        for t in range(1, T):
            acc = acc + exps[b, t] * lane_of(share, t * B + b)
        imp_part[b // 4, pl.ds(b % 4, 1)] = jnp.sum(acc, axis=0, keepdims=True)
    y_copies = []
    for d in range(1, NY):
        copy = remote(
            imp_part.at[lax.rem(my + d, NY)], imp_in.at[d - 1], y_s.at[d - 1], y_r.at[d - 1], y_dev(d)
        )
        copy.start()
        y_copies.append(copy)

    def take_z(d):
        gz[d].wait_recv()
        forward_x(d)
        forward_core(d, 0)

    def take_x(d, dx):
        gx[d, dx].wait_recv()
        forward_core(d, dx)

    take_z(1)
    take_z(7)
    take_x(0, 1)
    take_x(0, 3)
    take_z(2)
    take_z(6)
    take_x(0, 2)
    take_z(3)
    take_z(5)
    take_z(4)
    for copy in y_copies:
        copy.wait_recv()
    imp_ref[...] = imp_part[my] + imp_in[0] + imp_in[1] + imp_in[2]
    for d in (1, 7, 2, 6, 3, 5, 4):
        for dx in (1, 3, 2):
            take_x(d, dx)
    for d in (0, 1, 7, 2, 6, 3, 5, 4):
        for dx in (0, 1, 3, 2):
            gc[d, dx].wait_recv()

    for t in range(T):
        for h in range(H):
            out_ref[t, :, h * D : (h + 1) * D] = gathered[t, :, h, :].astype(BF16)

    for copy in (
        [core_stat] + core_copies + x_stats + [c for r in x_copies for c in r]
        + z_stats + z_copies + y_copies + list(gz.values()) + list(gx.values()) + list(gc.values())
    ):
        copy.wait_send()


DECODE = T


def on_device(queries, cache_keys, stored_values, new_keys, decoded_values, keep_mask):
    any_space = pl.BlockSpec(memory_space=pltpu.MemorySpace.HBM)
    vmem = pl.BlockSpec(memory_space=pltpu.VMEM)
    dma = pltpu.SemaphoreType.DMA
    return pl.pallas_call(
        kernel,
        out_shape=(
            jax.ShapeDtypeStruct((T, B, H * D), BF16),
            jax.ShapeDtypeStruct((B // NY, S), F32),
        ),
        in_specs=[any_space] * 6,
        out_specs=(vmem, vmem),
        scratch_shapes=[
            pltpu.VMEM((T, B, H, D), BF16),
            pltpu.VMEM((B, KV, S, D), BF16),
            pltpu.VMEM((B, KV, S, D), BF16),
            pltpu.VMEM((T, 2, KV, D), BF16),
            pltpu.VMEM((T, 2, KV, D), BF16),
            pltpu.VMEM((B, S), jnp.int32),
            pltpu.VMEM((B, T, H, D), F32),
            pltpu.VMEM((B, T, H, S), F32),
            pltpu.VMEM((H, D), F32),
            pltpu.VMEM((NZ, 2, NX, H, D), F32),
            pltpu.VMEM((NZ, NX, 2, H, D), F32),
            pltpu.VMEM((NZ, NX - 1, 2, H, D), F32),
            pltpu.VMEM((NZ, 2, H, D), F32),
            pltpu.VMEM((NZ - 1, 2, H, D), F32),
            pltpu.VMEM((T, B, H, D), F32),
            pltpu.VMEM((NY, B // NY, S), F32),
            pltpu.VMEM((NY - 1, B // NY, S), F32),
            pltpu.VMEM((2, H, D), F32),
            pltpu.VMEM((2, H, D), F32),
            pltpu.VMEM((2, H, D), F32),
            pltpu.VMEM((NX - 1, 2, H, D), F32),
            pltpu.VMEM((2, H, D), F32),
            pltpu.VMEM((NZ - 1, 2, H, D), F32),
            dma((4,)),
            dma((2, B)),
            dma, dma, dma((NZ,)), dma((NZ,)),
            dma((NX - 1,)), dma((NX - 1,)), dma((NZ, NX - 1)), dma((NZ, NX - 1)),
            dma((NZ - 1,)), dma((NZ - 1,)), dma((NZ - 1,)), dma((NZ - 1,)),
            dma((NY - 1,)), dma((NY - 1,)),
            dma((NZ - 1,)), dma((NZ - 1,)), dma((NZ, NX - 1)), dma((NZ, NX - 1)),
            dma((NZ, NX)), dma((NZ, NX)),
        ],
        compiler_params=pltpu.CompilerParams(
            collective_id=0, has_side_effects=True, vmem_limit_bytes=63 << 20
        ),
    )(queries, cache_keys, stored_values, new_keys, decoded_values, keep_mask)


def solution(mesh):
    finer = Mesh(
        mesh.devices.reshape(mesh.shape["head"], NX, NZ, NC), ("head", "seq_0", "seq_1", "seq_2")
    )
    seq = ("seq_0", "seq_1", "seq_2")
    in_specs = (
        P(None, None, "head", None),
        P(None, "head", seq, None),
        P(None, "head", seq, None),
        P(None, None, "head", None),
        P(None, None, "head", None),
        P(None, seq),
    )
    out_specs = (P(None, None, "head"), P("head", seq))
    return jax.shard_map(
        on_device, mesh=finer, in_specs=in_specs, out_specs=out_specs, check_vma=False
    )
```

```python
import jax
import jax.numpy as jnp
from jax import lax
from jax.experimental import pallas as pl
from jax.experimental.pallas import tpu as pltpu
from jax.sharding import Mesh
from jax.sharding import PartitionSpec as P

F32 = jnp.float32
BF16 = jnp.bfloat16
MESH = pl.DeviceIdType.MESH
SCALE = 1.0 / 12.0
FAR_BELOW = -1e30

T, B, H, D = 8, 16, 8, 128
KV = 4
S = 128
NY, NX, NZ, NC = 4, 4, 8, 2
FAR_FIRST = (4, 3, 5, 2, 6, 1, 7)
SLOT = [(d + 2) % NZ for d in range(NZ)]
FAR, NEAR = (5, 3), (0, 5)
HEADS_ALL = 32
CONTEXT = S * NX * NZ * NC


def lane_of(tile, lane):
    return jnp.broadcast_to(tile[:, lane : lane + 1], (H, D))


def to_front(tile, lane):
    return pltpu.roll(tile, lax.rem(128 - lane, 128), 1)


def expand_heads(rows):
    sub = lax.broadcasted_iota(jnp.int32, (H, D), 0)
    out = jnp.broadcast_to(rows[KV - 1 : KV], (H, D))
    for k in range(KV - 2, -1, -1):
        out = jnp.where(sub < 2 * (k + 1), jnp.broadcast_to(rows[k : k + 1], (H, D)), out)
    return out


def kernel(
    q_hbm, k_hbm, v_hbm, nk_hbm, nv_hbm, mask_hbm,
    out_ref, imp_ref,
    q_ref, k_ref, v_ref, nk_ref, nv_ref, mask_ref,
    sums, exps, peaks, core_in, pair, x_in, z_out, z_in, gathered, imp_part, imp_in,
    f_pair, f_x, stat_own, stat_core, stat_pair, stat_x, stat_group, stat_z,
    in_sem, chunk_sem,
    cs_s, cs_r, cd_s, cd_r, xs_s, xs_r, xd_s, xd_r, zs_s, zs_r, zd_s, zd_r, y_s, y_r,
    gz_s, gz_r, gx_s, gx_r, gc_s, gc_r,
):
    my = lax.axis_index("head")
    mx = lax.axis_index("seq_0")
    mz = lax.axis_index("seq_1")
    mc = lax.axis_index("seq_2")
    other = 1 - mc
    t_half = NX * mc
    t_own = t_half + mx
    base = lax.rem(mz + NZ - 2, NZ)

    def core_dev():
        return {"seq_2": other}

    def x_dev(d):
        return {"seq_0": lax.rem(mx + d, NX)}

    def z_dev(d):
        return {"seq_1": lax.rem(mz + d, NZ)}

    def y_dev(d):
        return {"head": lax.rem(my + d, NY)}

    started = []

    def remote(src, dst, ss, rs, dev):
        copy = pltpu.make_async_remote_copy(
            src_ref=src, dst_ref=dst, send_sem=ss, recv_sem=rs, device_id=dev, device_id_type=MESH
        )
        copy.start()
        started.append(copy)
        return copy

    barrier = pltpu.get_barrier_semaphore()
    partners = (
        [z_dev(d) for d in FAR_FIRST]
        + [x_dev(d) for d in (2, 1, 3)]
        + [y_dev(d) for d in (2, 1, 3)]
        + [core_dev()]
    )
    for dev in partners:
        pl.semaphore_signal(barrier, inc=1, device_id=dev, device_id_type=MESH)

    def chunk_loads(slot):
        rows = pl.ds(2 * lax.rem(base + slot, NZ), 2)
        mine = pl.ds(2 * slot, 2)
        return [
            pltpu.make_async_copy(q_hbm.at[:, rows], q_ref.at[:, mine], chunk_sem.at[0, slot]),
            pltpu.make_async_copy(k_hbm.at[rows], k_ref.at[mine], chunk_sem.at[1, slot]),
            pltpu.make_async_copy(v_hbm.at[rows], v_ref.at[mine], chunk_sem.at[2, slot]),
        ]

    b_own = 2 * mz
    small = [
        pltpu.make_async_copy(mask_hbm, mask_ref, in_sem.at[0]),
        pltpu.make_async_copy(nk_hbm.at[:, pl.ds(b_own, 2)], nk_ref, in_sem.at[1]),
        pltpu.make_async_copy(nv_hbm.at[:, pl.ds(b_own, 2)], nv_ref, in_sem.at[2]),
    ]
    small[0].start()
    loads = {slot: chunk_loads(slot) for slot in range(NZ)}
    batches = ((4, 5, 6, 7), (0, 1, 2, 3))
    for slots in batches:
        for slot in slots:
            for copy in loads[slot]:
                copy.start()
    for copy in small[1:]:
        copy.start()
    small[0].wait()

    lane = lax.broadcasted_iota(jnp.int32, (H, D), 1)
    row_kv = lax.rem(lax.broadcasted_iota(jnp.int32, (T * H, S), 0), H) // 2

    zero = jnp.zeros((H, D), F32)
    block_peak, block_total = zero, zero
    for slots in batches:
        for slot in slots:
            for copy in loads[slot]:
                copy.wait()
        rows = [2 * slot + i for slot in slots for i in range(2)]
        scores = []
        for r in rows:
            q = q_ref[:, r].astype(F32).reshape(T * H, D).astype(BF16)
            wide = lax.dot_general(
                q, k_ref[r].reshape(KV * S, D), (((1,), (1,)), ((), ())), preferred_element_type=F32
            )
            s = wide[:, (KV - 1) * S :]
            for k in range(KV - 2, -1, -1):
                s = jnp.where(row_kv == k, wide[:, k * S : (k + 1) * S], s)
            scores.append(s * SCALE)
        weights = []
        for r, s in zip(rows, scores):
            b = lax.rem(2 * base + r, B)
            keep = jnp.broadcast_to(mask_ref[pl.ds(b, 1), :], (T * H, S)) > 0
            m = jnp.max(jnp.where(keep, s, FAR_BELOW), axis=1, keepdims=True)
            e = jnp.where(keep, jnp.exp(s - m), 0.0)
            total = jnp.sum(e, axis=1, keepdims=True)
            exps[r] = e.reshape(T, H, S)
            weights.append(e)
            for t in range(T):
                here = lane == t * B + r
                part = slice(t * H, (t + 1) * H)
                block_peak = jnp.where(here, jnp.broadcast_to(m[part], (H, D)), block_peak)
                block_total = jnp.where(here, jnp.broadcast_to(total[part], (H, D)), block_total)
        for r, e in zip(rows, weights):
            wide = jnp.concatenate(
                [jnp.where(row_kv == k, e, 0.0).astype(BF16) for k in range(KV)], axis=1
            )
            o = jnp.dot(wide, v_ref[r].reshape(KV * S, D), preferred_element_type=F32)
            sums[r] = o.reshape(T, H, D)
    peaks[...] = block_peak

    peak_tile, total_tile = block_peak, block_total
    for copy in small[1:]:
        copy.wait()
    for i in range(2):
        r = 2 * SLOT[0] + i
        here = lane == t_own * B + r
        q = q_ref[t_own, r].astype(F32)
        ns = []
        for j in range(T):
            prod = q * expand_heads(nk_ref[j, i].astype(F32))
            sj = jnp.broadcast_to(jnp.sum(prod, axis=1, keepdims=True), (H, D)) * SCALE
            ns.append(jnp.where(j <= t_own, sj, FAR_BELOW))
        new_peak = ns[0]
        for j in range(1, T):
            new_peak = jnp.maximum(new_peak, ns[j])
        new_total, new_sum = zero, zero
        for j in range(T):
            ej = jnp.where(j <= t_own, jnp.exp(ns[j] - new_peak), 0.0)
            new_total = new_total + ej
            new_sum = new_sum + ej.astype(BF16).astype(F32) * expand_heads(nv_ref[j, i].astype(F32))
        old_peak = jnp.max(jnp.where(here, block_peak, -3e38), axis=1, keepdims=True)
        old_total = jnp.sum(jnp.where(here, block_total, 0.0), axis=1, keepdims=True)
        old_peak = jnp.broadcast_to(old_peak, (H, D))
        old_total = jnp.broadcast_to(old_total, (H, D))
        both = jnp.maximum(old_peak, new_peak)
        f_old = jnp.exp(old_peak - both)
        f_new = jnp.exp(new_peak - both)
        sums[r, t_own] = sums[r, t_own] * f_old + new_sum * f_new
        peak_tile = jnp.where(here, both, peak_tile)
        total_tile = jnp.where(here, old_total * f_old + new_total * f_new, total_tile)
    stat_own[0] = peak_tile
    stat_own[1] = total_tile

    pl.semaphore_wait(barrier, len(partners))

    core_stat = remote(stat_own, stat_core, cs_s, cs_r, core_dev())
    core_copies = []
    for g, (first, count) in enumerate((FAR, NEAR)):
        rows = pl.ds(2 * first, 2 * count)
        core_copies.append(
            remote(
                sums.at[rows, pl.ds(NX * other, NX)], core_in.at[rows], cd_s.at[g], cd_r.at[g],
                core_dev(),
            )
        )
    core_stat.wait_recv()
    peak_c, total_c = stat_core[0], stat_core[1]
    pair_peak = jnp.maximum(peak_tile, peak_c)
    f_own = jnp.exp(peak_tile - pair_peak)
    f_core = jnp.exp(peak_c - pair_peak)
    pair_total = total_tile * f_own + total_c * f_core
    stat_pair[0] = pair_peak
    stat_pair[1] = pair_total

    x_stats = []
    for d in (2, 1, 3):
        x_stats.append(
            remote(stat_pair, stat_x.at[d - 1], xs_s.at[d - 1], xs_r.at[d - 1], x_dev(d))
        )
    fo = to_front(f_own, t_half * B)
    fc = to_front(f_core, t_half * B)
    for first, count in (FAR, NEAR):
        for tl in range(NX):
            for r in range(2 * first, 2 * (first + count)):
                f_pair[0, tl, r] = lane_of(fo, tl * B + r)
                f_pair[1, tl, r] = lane_of(fc, tl * B + r)
    x_copies = []
    for g, (first, count) in enumerate((FAR, NEAR)):
        core_copies[g].wait_recv()
        for tl in range(NX):
            for r in range(2 * first, 2 * (first + count)):
                pair[tl, r] = (
                    sums[r, t_half + tl] * f_pair[0, tl, r] + core_in[r, tl] * f_pair[1, tl, r]
                )
        rows = pl.ds(2 * first, 2 * count)
        x_copies.append(
            [
                remote(
                    pair.at[lax.rem(mx + d, NX), rows], x_in.at[d - 1, rows],
                    xd_s.at[g, d - 1], xd_r.at[g, d - 1], x_dev(d),
                )
                for d in (2, 1, 3)
            ]
        )
    for copy in x_stats:
        copy.wait_recv()
    group_peak = pair_peak
    for d in range(1, NX):
        group_peak = jnp.maximum(group_peak, stat_x[d - 1, 0])
    factors = [jnp.exp(pair_peak - group_peak)]
    group_total = pair_total * factors[0]
    for d in range(1, NX):
        f = jnp.exp(stat_x[d - 1, 0] - group_peak)
        factors.append(f)
        group_total = group_total + stat_x[d - 1, 1] * f

    shift = 2 * base
    in_row = lax.rem(lane, B)

    def by_row(tile):
        return jnp.where(
            in_row >= shift, pltpu.roll(tile, shift, 1), pltpu.roll(tile, lax.rem(shift + 112, 128), 1)
        )

    def by_slot(tile):
        return jnp.where(
            in_row < B - shift,
            pltpu.roll(tile, lax.rem(128 - shift, 128), 1),
            pltpu.roll(tile, lax.rem(144 - shift, 128), 1),
        )

    group_peak = by_row(group_peak)
    group_total = by_row(group_total)
    stat_group[0] = group_peak
    stat_group[1] = group_total
    z_stats = [
        remote(stat_group, stat_z.at[d - 1], zs_s.at[d - 1], zs_r.at[d - 1], z_dev(d))
        for d in FAR_FIRST
    ]
    for d in range(NX):
        f = to_front(factors[d], t_own * B)
        for r in range(B):
            f_x[d, r] = lane_of(f, r)
    z_copies = []
    for g, sends in enumerate(((4, 3, 5), (2, 6, 1, 7, 0))):
        for copy in x_copies[g]:
            copy.wait_recv()
        for d in sends:
            for i in range(2):
                r = 2 * SLOT[d] + i
                acc = pair[mx, r] * f_x[0, r]
                for dx in range(1, NX):
                    acc = acc + x_in[dx - 1, r] * f_x[dx, r]
                z_out[SLOT[d], i] = acc
            if d > 0:
                z_copies.append(
                    remote(
                        z_out.at[SLOT[d]], z_in.at[d - 1], zd_s.at[d - 1], zd_r.at[d - 1], z_dev(d)
                    )
                )
    for copy in z_stats:
        copy.wait_recv()
    peak = group_peak
    for d in range(1, NZ):
        peak = jnp.maximum(peak, stat_z[d - 1, 0])
    factors = [jnp.exp(group_peak - peak)]
    total = group_total * factors[0]
    for d in range(1, NZ):
        f = jnp.exp(stat_z[d - 1, 0] - peak)
        factors.append(f)
        total = total + stat_z[d - 1, 1] * f
    inverse = 1.0 / total
    front = [to_front(f * inverse, t_own * B + b_own) for f in factors]
    scale = [[lane_of(f, i) for f in front] for i in range(2)]
    share = jnp.exp(peaks[...] - by_slot(peak)) * by_slot(inverse) * (CONTEXT / (T * HEADS_ALL))
    for copy in z_copies:
        copy.wait_recv()
    for i in range(2):
        acc = z_out[SLOT[0], i] * scale[i][0]
        for d in range(1, NZ):
            acc = acc + z_in[d - 1, i] * scale[i][d]
        gathered[t_own, 2 * (base + SLOT[0]) + i] = acc

    own = gathered.at[t_own, pl.ds(2 * (base + SLOT[0]), 2)]
    gz = {}
    for d in FAR_FIRST:
        place = lax.rem(mz + d + NZ - 2, NZ) + SLOT[NZ - d]
        gz[d] = remote(
            own, gathered.at[t_own, pl.ds(2 * place, 2)], gz_s.at[d - 1], gz_r.at[d - 1], z_dev(d)
        )

    for r in range(B):
        acc = exps[r, 0] * lane_of(share, r)
        for t in range(1, T):
            acc = acc + exps[r, t] * lane_of(share, t * B + r)
        b = lax.rem(2 * base + r, B)
        imp_part[b // 4, pl.ds(lax.rem(b, 4), 1)] = jnp.sum(acc, axis=0, keepdims=True)
    y_copies = []
    for d in (2, 1, 3):
        y_copies.append(
            remote(
                imp_part.at[lax.rem(my + d, NY)], imp_in.at[d - 1], y_s.at[d - 1], y_r.at[d - 1],
                y_dev(d),
            )
        )

    spans = (NEAR, FAR)
    gx, gc = {}, []

    def span_of(t, g):
        first, count = spans[g]
        return gathered.at[t, pl.ds(2 * (base + first), 2 * count)]

    def forward_core(g, dx):
        span = span_of(t_half + lax.rem(mx + NX - dx, NX), g)
        gc.append(remote(span, span, gc_s.at[g, dx], gc_r.at[g, dx], core_dev()))

    for g, arrivals in enumerate(((1, 7, 2, 6), (3, 5, 4))):
        for d in arrivals:
            gz[d].wait_recv()
        span = span_of(t_own, g)
        for dx in (2, 1, 3):
            gx[g, dx] = remote(span, span, gx_s.at[g, dx - 1], gx_r.at[g, dx - 1], x_dev(dx))
        forward_core(g, 0)

    for copy in y_copies:
        copy.wait_recv()
    imp_ref[...] = imp_part[my] + imp_in[0] + imp_in[1] + imp_in[2]

    for g in range(2):
        for dx in (1, 3, 2):
            gx[g, dx].wait_recv()
            forward_core(g, dx)

    wrapped = lax.broadcasted_iota(jnp.int32, (B, D), 0) < shift

    def emit(half):
        for tl in range(NX):
            t = NX * half + tl
            for h in range(H):
                straight = gathered[t, 0:B, h, :]
                beyond = gathered[t, B : 2 * B, h, :]
                out_ref[t, :, h * D : (h + 1) * D] = jnp.where(wrapped, beyond, straight).astype(BF16)

    emit(mc)
    for copy in gc:
        copy.wait_recv()
    emit(other)

    for copy in started:
        copy.wait_send()


def on_device(queries, cache_keys, stored_values, new_keys, decoded_values, keep_mask):
    any_space = pl.BlockSpec(memory_space=pltpu.MemorySpace.HBM)
    vmem = pl.BlockSpec(memory_space=pltpu.VMEM)
    dma = pltpu.SemaphoreType.DMA
    return pl.pallas_call(
        kernel,
        out_shape=(
            jax.ShapeDtypeStruct((T, B, H * D), BF16),
            jax.ShapeDtypeStruct((B // NY, S), F32),
        ),
        in_specs=[any_space] * 6,
        out_specs=(vmem, vmem),
        scratch_shapes=[
            pltpu.VMEM((T, B, H, D), BF16),
            pltpu.VMEM((B, KV, S, D), BF16),
            pltpu.VMEM((B, KV, S, D), BF16),
            pltpu.VMEM((T, 2, KV, D), BF16),
            pltpu.VMEM((T, 2, KV, D), BF16),
            pltpu.VMEM((B, S), jnp.int32),
            pltpu.VMEM((B, T, H, D), F32),
            pltpu.VMEM((B, T, H, S), F32),
            pltpu.VMEM((H, D), F32),
            pltpu.VMEM((B, NX, H, D), F32),
            pltpu.VMEM((NX, B, H, D), F32),
            pltpu.VMEM((NX - 1, B, H, D), F32),
            pltpu.VMEM((NZ, 2, H, D), F32),
            pltpu.VMEM((NZ - 1, 2, H, D), F32),
            pltpu.VMEM((T, 2 * B, H, D), F32),
            pltpu.VMEM((NY, B // NY, S), F32),
            pltpu.VMEM((NY - 1, B // NY, S), F32),
            pltpu.VMEM((2, NX, B, H, D), F32),
            pltpu.VMEM((NX, B, H, D), F32),
            pltpu.VMEM((2, H, D), F32),
            pltpu.VMEM((2, H, D), F32),
            pltpu.VMEM((2, H, D), F32),
            pltpu.VMEM((NX - 1, 2, H, D), F32),
            pltpu.VMEM((2, H, D), F32),
            pltpu.VMEM((NZ - 1, 2, H, D), F32),
            dma((3,)),
            dma((3, NZ)),
            dma, dma, dma((2,)), dma((2,)),
            dma((NX - 1,)), dma((NX - 1,)), dma((2, NX - 1)), dma((2, NX - 1)),
            dma((NZ - 1,)), dma((NZ - 1,)), dma((NZ - 1,)), dma((NZ - 1,)),
            dma((NY - 1,)), dma((NY - 1,)),
            dma((NZ - 1,)), dma((NZ - 1,)), dma((2, NX - 1)), dma((2, NX - 1)),
            dma((2, NX)), dma((2, NX)),
        ],
        compiler_params=pltpu.CompilerParams(
            collective_id=0, has_side_effects=True, vmem_limit_bytes=63 << 20
        ),
    )(queries, cache_keys, stored_values, new_keys, decoded_values, keep_mask)


def solution(mesh):
    finer = Mesh(
        mesh.devices.reshape(mesh.shape["head"], NX, NZ, NC), ("head", "seq_0", "seq_1", "seq_2")
    )
    seq = ("seq_0", "seq_1", "seq_2")
    in_specs = (
        P(None, None, "head", None),
        P(None, "head", seq, None),
        P(None, "head", seq, None),
        P(None, None, "head", None),
        P(None, None, "head", None),
        P(None, seq),
    )
    out_specs = (P(None, None, "head"), P("head", seq))
    return jax.shard_map(
        on_device, mesh=finer, in_specs=in_specs, out_specs=out_specs, check_vma=False
    )
```

```python
import jax
import jax.numpy as jnp
from jax import lax
from jax.experimental import pallas as pl
from jax.experimental.pallas import tpu as pltpu
from jax.sharding import Mesh
from jax.sharding import PartitionSpec as P

F32 = jnp.float32
BF16 = jnp.bfloat16
MESH = pl.DeviceIdType.MESH
SCALE = 1.0 / 12.0
FAR_BELOW = -1e30

T, B, H, D = 8, 16, 8, 128
KV = 4
S = 128
NY, NX, NZ, NC = 4, 4, 8, 2
FAR_FIRST = (4, 3, 5, 2, 6, 1, 7)
SLOT = [(d + 2) % NZ for d in range(NZ)]
FAR, NEAR = (5, 3), (0, 5)
HEADS_ALL = 32
CONTEXT = S * NX * NZ * NC


def lane_of(tile, lane):
    return jnp.broadcast_to(tile[:, lane : lane + 1], (H, D))


def to_front(tile, lane):
    return pltpu.roll(tile, lax.rem(128 - lane, 128), 1)


def expand_heads(rows):
    sub = lax.broadcasted_iota(jnp.int32, (H, D), 0)
    out = jnp.broadcast_to(rows[KV - 1 : KV], (H, D))
    for k in range(KV - 2, -1, -1):
        out = jnp.where(sub < 2 * (k + 1), jnp.broadcast_to(rows[k : k + 1], (H, D)), out)
    return out


def kernel(
    q_hbm, k_hbm, v_hbm, nk_hbm, nv_hbm, mask_hbm,
    out_ref, imp_ref,
    q_ref, k_ref, v_ref, nk_ref, nv_ref, mask_ref,
    sums, exps, peaks, core_in, pair, x_in, z_out, z_in, gathered, imp_part, imp_in,
    f_pair, f_x, stat_own, stat_core, stat_pair, stat_x, stat_group, stat_z,
    in_sem, chunk_sem,
    cs_s, cs_r, cd_s, cd_r, xs_s, xs_r, xd_s, xd_r, zs_s, zs_r, zd_s, zd_r, y_s, y_r,
    gz_s, gz_r, gx_s, gx_r, gc_s, gc_r,
):
    my = lax.axis_index("head")
    mx = lax.axis_index("seq_0")
    mz = lax.axis_index("seq_1")
    mc = lax.axis_index("seq_2")
    other = 1 - mc
    t_half = NX * mc
    t_own = t_half + mx
    base = lax.rem(mz + NZ - 2, NZ)

    def core_dev():
        return {"seq_2": other}

    def x_dev(d):
        return {"seq_0": lax.rem(mx + d, NX)}

    def z_dev(d):
        return {"seq_1": lax.rem(mz + d, NZ)}

    def y_dev(d):
        return {"head": lax.rem(my + d, NY)}

    started = []

    def remote(src, dst, ss, rs, dev):
        copy = pltpu.make_async_remote_copy(
            src_ref=src, dst_ref=dst, send_sem=ss, recv_sem=rs, device_id=dev, device_id_type=MESH
        )
        copy.start()
        started.append(copy)
        return copy

    barrier = pltpu.get_barrier_semaphore()
    partners = (
        [z_dev(d) for d in FAR_FIRST]
        + [x_dev(d) for d in (2, 1, 3)]
        + [y_dev(d) for d in (2, 1, 3)]
        + [core_dev()]
    )
    for dev in partners:
        pl.semaphore_signal(barrier, inc=1, device_id=dev, device_id_type=MESH)

    def chunk_loads(slot):
        rows = pl.ds(2 * lax.rem(base + slot, NZ), 2)
        mine = pl.ds(2 * slot, 2)
        return [
            pltpu.make_async_copy(q_hbm.at[:, rows], q_ref.at[:, mine], chunk_sem.at[0, slot]),
            pltpu.make_async_copy(k_hbm.at[rows], k_ref.at[mine], chunk_sem.at[1, slot]),
            pltpu.make_async_copy(v_hbm.at[rows], v_ref.at[mine], chunk_sem.at[2, slot]),
        ]

    b_own = 2 * mz
    small = [
        pltpu.make_async_copy(mask_hbm, mask_ref, in_sem.at[0]),
        pltpu.make_async_copy(nk_hbm.at[:, pl.ds(b_own, 2)], nk_ref, in_sem.at[1]),
        pltpu.make_async_copy(nv_hbm.at[:, pl.ds(b_own, 2)], nv_ref, in_sem.at[2]),
    ]
    small[0].start()
    loads = {slot: chunk_loads(slot) for slot in range(NZ)}
    batches = ((4, 5, 6, 7), (0, 1, 2, 3))
    for slots in batches:
        for slot in slots:
            for copy in loads[slot]:
                copy.start()
    for copy in small[1:]:
        copy.start()
    small[0].wait()

    lane = lax.broadcasted_iota(jnp.int32, (H, D), 1)
    row_kv = lax.rem(lax.broadcasted_iota(jnp.int32, (T * H, S), 0), H) // 2

    zero = jnp.zeros((H, D), F32)
    block_peak, block_total = zero, zero
    for slots in batches:
        for slot in slots:
            for copy in loads[slot]:
                copy.wait()
        rows = [2 * slot + i for slot in slots for i in range(2)]
        scores = []
        for r in rows:
            q = q_ref[:, r].astype(F32).reshape(T * H, D).astype(BF16)
            wide = lax.dot_general(
                q, k_ref[r].reshape(KV * S, D), (((1,), (1,)), ((), ())), preferred_element_type=F32
            )
            s = wide[:, (KV - 1) * S :]
            for k in range(KV - 2, -1, -1):
                s = jnp.where(row_kv == k, wide[:, k * S : (k + 1) * S], s)
            scores.append(s * SCALE)
        weights = []
        for r, s in zip(rows, scores):
            b = lax.rem(2 * base + r, B)
            keep = jnp.broadcast_to(mask_ref[pl.ds(b, 1), :], (T * H, S)) > 0
            m = jnp.max(jnp.where(keep, s, FAR_BELOW), axis=1, keepdims=True)
            e = jnp.where(keep, jnp.exp(s - m), 0.0)
            total = jnp.sum(e, axis=1, keepdims=True)
            exps[r] = e.reshape(T, H, S)
            weights.append(e)
            for t in range(T):
                here = lane == t * B + r
                part = slice(t * H, (t + 1) * H)
                block_peak = jnp.where(here, jnp.broadcast_to(m[part], (H, D)), block_peak)
                block_total = jnp.where(here, jnp.broadcast_to(total[part], (H, D)), block_total)
        for r, e in zip(rows, weights):
            wide = jnp.concatenate(
                [jnp.where(row_kv == k, e, 0.0).astype(BF16) for k in range(KV)], axis=1
            )
            o = jnp.dot(wide, v_ref[r].reshape(KV * S, D), preferred_element_type=F32)
            sums[r] = o.reshape(T, H, D)
    peaks[...] = block_peak

    peak_tile, total_tile = block_peak, block_total
    for copy in small[1:]:
        copy.wait()
    for i in range(2):
        r = 2 * SLOT[0] + i
        here = lane == t_own * B + r
        q = q_ref[t_own, r].astype(F32)
        ns = []
        for j in range(T):
            prod = q * expand_heads(nk_ref[j, i].astype(F32))
            sj = jnp.broadcast_to(jnp.sum(prod, axis=1, keepdims=True), (H, D)) * SCALE
            ns.append(jnp.where(j <= t_own, sj, FAR_BELOW))
        new_peak = ns[0]
        for j in range(1, T):
            new_peak = jnp.maximum(new_peak, ns[j])
        new_total, new_sum = zero, zero
        for j in range(T):
            ej = jnp.where(j <= t_own, jnp.exp(ns[j] - new_peak), 0.0)
            new_total = new_total + ej
            new_sum = new_sum + ej.astype(BF16).astype(F32) * expand_heads(nv_ref[j, i].astype(F32))
        old_peak = jnp.max(jnp.where(here, block_peak, -3e38), axis=1, keepdims=True)
        old_total = jnp.sum(jnp.where(here, block_total, 0.0), axis=1, keepdims=True)
        old_peak = jnp.broadcast_to(old_peak, (H, D))
        old_total = jnp.broadcast_to(old_total, (H, D))
        both = jnp.maximum(old_peak, new_peak)
        f_old = jnp.exp(old_peak - both)
        f_new = jnp.exp(new_peak - both)
        sums[r, t_own] = sums[r, t_own] * f_old + new_sum * f_new
        peak_tile = jnp.where(here, both, peak_tile)
        total_tile = jnp.where(here, old_total * f_old + new_total * f_new, total_tile)
    stat_own[0] = peak_tile
    stat_own[1] = total_tile

    pl.semaphore_wait(barrier, len(partners))

    core_stat = remote(stat_own, stat_core, cs_s, cs_r, core_dev())
    core_copies = []
    for g, (first, count) in enumerate((FAR, NEAR)):
        rows = pl.ds(2 * first, 2 * count)
        core_copies.append(
            remote(
                sums.at[rows, pl.ds(NX * other, NX)], core_in.at[rows], cd_s.at[g], cd_r.at[g],
                core_dev(),
            )
        )
    core_stat.wait_recv()
    peak_c, total_c = stat_core[0], stat_core[1]
    pair_peak = jnp.maximum(peak_tile, peak_c)
    f_own = jnp.exp(peak_tile - pair_peak)
    f_core = jnp.exp(peak_c - pair_peak)
    pair_total = total_tile * f_own + total_c * f_core
    stat_pair[0] = pair_peak
    stat_pair[1] = pair_total

    x_stats = []
    for d in (2, 1, 3):
        x_stats.append(
            remote(stat_pair, stat_x.at[d - 1], xs_s.at[d - 1], xs_r.at[d - 1], x_dev(d))
        )
    fo = to_front(f_own, t_half * B)
    fc = to_front(f_core, t_half * B)
    for first, count in (FAR, NEAR):
        for tl in range(NX):
            for r in range(2 * first, 2 * (first + count)):
                f_pair[0, tl, r] = lane_of(fo, tl * B + r)
                f_pair[1, tl, r] = lane_of(fc, tl * B + r)
    x_copies = []
    for g, (first, count) in enumerate((FAR, NEAR)):
        core_copies[g].wait_recv()
        for tl in range(NX):
            for r in range(2 * first, 2 * (first + count)):
                pair[tl, r] = (
                    sums[r, t_half + tl] * f_pair[0, tl, r] + core_in[r, tl] * f_pair[1, tl, r]
                )
        rows = pl.ds(2 * first, 2 * count)
        x_copies.append(
            [
                remote(
                    pair.at[lax.rem(mx + d, NX), rows], x_in.at[d - 1, rows],
                    xd_s.at[g, d - 1], xd_r.at[g, d - 1], x_dev(d),
                )
                for d in (2, 1, 3)
            ]
        )
    for copy in x_stats:
        copy.wait_recv()
    group_peak = pair_peak
    for d in range(1, NX):
        group_peak = jnp.maximum(group_peak, stat_x[d - 1, 0])
    factors = [jnp.exp(pair_peak - group_peak)]
    group_total = pair_total * factors[0]
    for d in range(1, NX):
        f = jnp.exp(stat_x[d - 1, 0] - group_peak)
        factors.append(f)
        group_total = group_total + stat_x[d - 1, 1] * f

    shift = 2 * base
    in_row = lax.rem(lane, B)

    def by_row(tile):
        return jnp.where(
            in_row >= shift, pltpu.roll(tile, shift, 1), pltpu.roll(tile, lax.rem(shift + 112, 128), 1)
        )

    def by_slot(tile):
        return jnp.where(
            in_row < B - shift,
            pltpu.roll(tile, lax.rem(128 - shift, 128), 1),
            pltpu.roll(tile, lax.rem(144 - shift, 128), 1),
        )

    group_peak = by_row(group_peak)
    group_total = by_row(group_total)
    stat_group[0] = group_peak
    stat_group[1] = group_total
    z_stats = [
        remote(stat_group, stat_z.at[d - 1], zs_s.at[d - 1], zs_r.at[d - 1], z_dev(d))
        for d in FAR_FIRST
    ]
    for d in range(NX):
        f = to_front(factors[d], t_own * B)
        for r in range(B):
            f_x[d, r] = lane_of(f, r)
    z_copies = []
    for g, sends in enumerate(((4, 3, 5), (2, 6, 1, 7, 0))):
        for copy in x_copies[g]:
            copy.wait_recv()
        for d in sends:
            for i in range(2):
                r = 2 * SLOT[d] + i
                acc = pair[mx, r] * f_x[0, r]
                for dx in range(1, NX):
                    acc = acc + x_in[dx - 1, r] * f_x[dx, r]
                z_out[SLOT[d], i] = acc
            if d > 0:
                z_copies.append(
                    remote(
                        z_out.at[SLOT[d]], z_in.at[d - 1], zd_s.at[d - 1], zd_r.at[d - 1], z_dev(d)
                    )
                )
    for copy in z_stats:
        copy.wait_recv()
    peak = group_peak
    for d in range(1, NZ):
        peak = jnp.maximum(peak, stat_z[d - 1, 0])
    factors = [jnp.exp(group_peak - peak)]
    total = group_total * factors[0]
    for d in range(1, NZ):
        f = jnp.exp(stat_z[d - 1, 0] - peak)
        factors.append(f)
        total = total + stat_z[d - 1, 1] * f
    inverse = 1.0 / total
    front = [to_front(f * inverse, t_own * B + b_own) for f in factors]
    scale = [[lane_of(f, i) for f in front] for i in range(2)]
    share = jnp.exp(peaks[...] - by_slot(peak)) * by_slot(inverse) * (CONTEXT / (T * HEADS_ALL))
    for copy in z_copies:
        copy.wait_recv()
    for i in range(2):
        acc = z_out[SLOT[0], i] * scale[i][0]
        for d in range(1, NZ):
            acc = acc + z_in[d - 1, i] * scale[i][d]
        gathered[t_own, 2 * (base + SLOT[0]) + i] = acc

    own = gathered.at[t_own, pl.ds(2 * (base + SLOT[0]), 2)]
    gz = {}
    for d in FAR_FIRST:
        place = lax.rem(mz + d + NZ - 2, NZ) + SLOT[NZ - d]
        gz[d] = remote(
            own, gathered.at[t_own, pl.ds(2 * place, 2)], gz_s.at[d - 1], gz_r.at[d - 1], z_dev(d)
        )

    for r in range(B):
        acc = exps[r, 0] * lane_of(share, r)
        for t in range(1, T):
            acc = acc + exps[r, t] * lane_of(share, t * B + r)
        b = lax.rem(2 * base + r, B)
        imp_part[b // 4, pl.ds(lax.rem(b, 4), 1)] = jnp.sum(acc, axis=0, keepdims=True)
    y_copies = []
    for d in (2, 1, 3):
        y_copies.append(
            remote(
                imp_part.at[lax.rem(my + d, NY)], imp_in.at[d - 1], y_s.at[d - 1], y_r.at[d - 1],
                y_dev(d),
            )
        )

    spans = (NEAR, FAR)
    gx, gc = {}, []

    def span_of(t, g):
        first, count = spans[g]
        return gathered.at[t, pl.ds(2 * (base + first), 2 * count)]

    def forward_core(g, dx):
        span = span_of(t_half + lax.rem(mx + NX - dx, NX), g)
        gc.append(remote(span, span, gc_s.at[g, dx], gc_r.at[g, dx], core_dev()))

    for g, arrivals in enumerate(((1, 7, 2, 6), (3, 5, 4))):
        for d in arrivals:
            gz[d].wait_recv()
        span = span_of(t_own, g)
        for dx in (2, 1, 3):
            gx[g, dx] = remote(span, span, gx_s.at[g, dx - 1], gx_r.at[g, dx - 1], x_dev(dx))
        forward_core(g, 0)

    for copy in y_copies:
        copy.wait_recv()
    imp_ref[...] = imp_part[my] + imp_in[0] + imp_in[1] + imp_in[2]

    for g in range(2):
        for dx in (1, 3, 2):
            gx[g, dx].wait_recv()
            forward_core(g, dx)

    wrapped = lax.broadcasted_iota(jnp.int32, (B, D), 0) < shift

    def emit(half):
        for tl in range(NX):
            t = NX * half + tl
            for h in range(H):
                straight = gathered[t, 0:B, h, :]
                beyond = gathered[t, B : 2 * B, h, :]
                out_ref[t, :, h * D : (h + 1) * D] = jnp.where(wrapped, beyond, straight).astype(BF16)

    emit(mc)
    for copy in gc:
        copy.wait_recv()
    emit(other)

    for copy in started:
        copy.wait_send()


def store(attended, importance, attended_out, importance_out, sem):
    copies = [
        pltpu.make_async_copy(attended, attended_out, sem.at[0]),
        pltpu.make_async_copy(importance, importance_out, sem.at[1]),
    ]
    for copy in copies:
        copy.start()
    for copy in copies:
        copy.wait()


def on_device(queries, cache_keys, stored_values, new_keys, decoded_values, keep_mask):
    any_space = pl.BlockSpec(memory_space=pl.ANY)
    vmem = pl.BlockSpec(memory_space=pltpu.VMEM)
    dma = pltpu.SemaphoreType.DMA
    attended, importance = pl.pallas_call(
        kernel,
        out_shape=(pltpu.VMEM((T, B, H * D), BF16), pltpu.VMEM((B // NY, S), F32)),
        in_specs=[any_space] * 6,
        out_specs=(vmem, vmem),
        scratch_shapes=[
            pltpu.VMEM((T, B, H, D), BF16),
            pltpu.VMEM((B, KV, S, D), BF16),
            pltpu.VMEM((B, KV, S, D), BF16),
            pltpu.VMEM((T, 2, KV, D), BF16),
            pltpu.VMEM((T, 2, KV, D), BF16),
            pltpu.VMEM((B, S), jnp.int32),
            pltpu.VMEM((B, T, H, D), F32),
            pltpu.VMEM((B, T, H, S), F32),
            pltpu.VMEM((H, D), F32),
            pltpu.VMEM((B, NX, H, D), F32),
            pltpu.VMEM((NX, B, H, D), F32),
            pltpu.VMEM((NX - 1, B, H, D), F32),
            pltpu.VMEM((NZ, 2, H, D), F32),
            pltpu.VMEM((NZ - 1, 2, H, D), F32),
            pltpu.VMEM((T, 2 * B, H, D), F32),
            pltpu.VMEM((NY, B // NY, S), F32),
            pltpu.VMEM((NY - 1, B // NY, S), F32),
            pltpu.VMEM((2, NX, B, H, D), F32),
            pltpu.VMEM((NX, B, H, D), F32),
            pltpu.VMEM((2, H, D), F32),
            pltpu.VMEM((2, H, D), F32),
            pltpu.VMEM((2, H, D), F32),
            pltpu.VMEM((NX - 1, 2, H, D), F32),
            pltpu.VMEM((2, H, D), F32),
            pltpu.VMEM((NZ - 1, 2, H, D), F32),
            dma((3,)),
            dma((3, NZ)),
            dma, dma, dma((2,)), dma((2,)),
            dma((NX - 1,)), dma((NX - 1,)), dma((2, NX - 1)), dma((2, NX - 1)),
            dma((NZ - 1,)), dma((NZ - 1,)), dma((NZ - 1,)), dma((NZ - 1,)),
            dma((NY - 1,)), dma((NY - 1,)),
            dma((NZ - 1,)), dma((NZ - 1,)), dma((2, NX - 1)), dma((2, NX - 1)),
            dma((2, NX)), dma((2, NX)),
        ],
        compiler_params=pltpu.CompilerParams(
            collective_id=0, has_side_effects=True, vmem_limit_bytes=63 << 20
        ),
    )(queries, cache_keys, stored_values, new_keys, decoded_values, keep_mask)
    return pl.pallas_call(
        store,
        out_shape=(
            jax.ShapeDtypeStruct((T, B, H * D), BF16),
            jax.ShapeDtypeStruct((B // NY, S), F32),
        ),
        in_specs=[vmem, vmem],
        out_specs=(any_space, any_space),
        scratch_shapes=[dma((2,))],
    )(
        pltpu.with_memory_space_constraint(attended, pltpu.MemorySpace.VMEM),
        pltpu.with_memory_space_constraint(importance, pltpu.MemorySpace.VMEM),
    )


def solution(mesh):
    finer = Mesh(
        mesh.devices.reshape(mesh.shape["head"], NX, NZ, NC), ("head", "seq_0", "seq_1", "seq_2")
    )
    seq = ("seq_0", "seq_1", "seq_2")
    in_specs = (
        P(None, None, "head", None),
        P(None, "head", seq, None),
        P(None, "head", seq, None),
        P(None, None, "head", None),
        P(None, None, "head", None),
        P(None, seq),
    )
    out_specs = (P(None, None, "head"), P("head", seq))
    return jax.shard_map(
        on_device, mesh=finer, in_specs=in_specs, out_specs=out_specs, check_vma=False
    )
```

```python
import jax
import jax.numpy as jnp
from jax import lax
from jax.experimental import pallas as pl
from jax.experimental.pallas import tpu as pltpu
from jax.sharding import Mesh
from jax.sharding import PartitionSpec as P

F32 = jnp.float32
BF16 = jnp.bfloat16
MESH = pl.DeviceIdType.MESH
SCALE = 1.0 / 12.0
FAR_BELOW = -1e30

T, B, H, D = 8, 16, 8, 128
KV = 4
S = 128
NY, NX, NZ, NC = 4, 4, 8, 2
FAR_FIRST = (4, 3, 5, 2, 6, 1, 7)
OUT = FAR_FIRST + (0,)
SLOT = [(d + 2) % NZ for d in range(NZ)]
ROWS = [(2 * m + i, d, 2 * SLOT[d] + i) for m, d in enumerate(OUT) for i in range(2)]
CORE_GROUPS = ((0, 3), (3, 5))
X_GROUPS = ((0, 3), (3, 2), (5, 2), (7, 1))
FAR, NEAR = (5, 3), (0, 5)
BACK_GROUPS = ((2, 1, ()), (3, 2, (7, 6)), (0, 2, (1, 2)), (5, 3, (3, 5, 4)))
HEADS_ALL = 32
CONTEXT = S * NX * NZ * NC


def lane_of(tile, lane):
    return jnp.broadcast_to(tile[:, lane : lane + 1], (H, D))


def to_front(tile, lane):
    return pltpu.roll(tile, lax.rem(128 - lane, 128), 1)


def expand_heads(rows):
    sub = lax.broadcasted_iota(jnp.int32, (H, D), 0)
    out = jnp.broadcast_to(rows[KV - 1 : KV], (H, D))
    for k in range(KV - 2, -1, -1):
        out = jnp.where(sub < 2 * (k + 1), jnp.broadcast_to(rows[k : k + 1], (H, D)), out)
    return out


def kernel(
    q_hbm, k_hbm, v_hbm, nk_hbm, nv_hbm, mask_hbm,
    out_ref, imp_ref,
    q_ref, k_ref, v_ref, nk_ref, nv_ref, mask_ref,
    sums, exps, peaks, core_in, pair, x_in, z_out, z_in, gathered, imp_part, imp_in,
    f_pair, f_x, stat_own, stat_core, stat_pair, stat_x, stat_group, stat_z,
    in_sem, chunk_sem,
    cs_s, cs_r, cd_s, cd_r, xs_s, xs_r, xd_s, xd_r, zs_s, zs_r, zd_s, zd_r, y_s, y_r,
    gz_s, gz_r, gx_s, gx_r, gc_s, gc_r, ready,
):
    my = lax.axis_index("head")
    mx = lax.axis_index("seq_0")
    mz = lax.axis_index("seq_1")
    mc = lax.axis_index("seq_2")
    other = 1 - mc
    t_half = NX * mc
    t_own = t_half + mx
    base = lax.rem(mz + NZ - 2, NZ)

    def core_dev():
        return {"seq_2": other}

    def x_dev(d):
        return {"seq_0": lax.rem(mx + d, NX)}

    def z_dev(d):
        return {"seq_1": lax.rem(mz + d, NZ)}

    def y_dev(d):
        return {"head": lax.rem(my + d, NY)}

    started = []

    def remote(src, dst, ss, rs, dev):
        copy = pltpu.make_async_remote_copy(
            src_ref=src, dst_ref=dst, send_sem=ss, recv_sem=rs, device_id=dev, device_id_type=MESH
        )
        copy.start()
        started.append(copy)
        return copy

    barrier = pltpu.get_barrier_semaphore()
    partners = (
        [z_dev(d) for d in (2, 6, 1, 7)]
        + [x_dev(d) for d in (2, 1, 3)]
        + [y_dev(d) for d in (2, 1, 3)]
        + [core_dev()]
    )
    for dev in partners:
        pl.semaphore_signal(barrier, inc=1, device_id=dev, device_id_type=MESH)

    def chunk_loads(m):
        rows = pl.ds(2 * lax.rem(mz + OUT[m], NZ), 2)
        mine = pl.ds(2 * m, 2)
        return [
            pltpu.make_async_copy(q_hbm.at[:, rows], q_ref.at[:, mine], chunk_sem.at[0, m]),
            pltpu.make_async_copy(k_hbm.at[rows], k_ref.at[mine], chunk_sem.at[1, m]),
            pltpu.make_async_copy(v_hbm.at[rows], v_ref.at[mine], chunk_sem.at[2, m]),
        ]

    def batch_row(d, i):
        return 2 * lax.rem(mz + d, NZ) + i

    b_own = 2 * mz
    small = [
        pltpu.make_async_copy(mask_hbm, mask_ref, in_sem.at[0]),
        pltpu.make_async_copy(nk_hbm.at[:, pl.ds(b_own, 2)], nk_ref, in_sem.at[1]),
        pltpu.make_async_copy(nv_hbm.at[:, pl.ds(b_own, 2)], nv_ref, in_sem.at[2]),
    ]
    small[0].start()
    loads = [chunk_loads(m) for m in range(NZ)]
    for copies in loads:
        for copy in copies:
            copy.start()
    for copy in small[1:]:
        copy.start()
    small[0].wait()

    lane = lax.broadcasted_iota(jnp.int32, (H, D), 1)
    row_kv = lax.rem(lax.broadcasted_iota(jnp.int32, (T * H, S), 0), H) // 2

    zero = jnp.zeros((H, D), F32)
    block_peak, block_total = zero, zero
    for batch in (range(0, 4), range(4, 8)):
        for m in batch:
            for copy in loads[m]:
                copy.wait()
        rows = ROWS[2 * batch[0] : 2 * batch[-1] + 2]
        scores = []
        for r, _, _ in rows:
            q = q_ref[:, r].astype(F32).reshape(T * H, D).astype(BF16)
            wide = lax.dot_general(
                q, k_ref[r].reshape(KV * S, D), (((1,), (1,)), ((), ())), preferred_element_type=F32
            )
            s = wide[:, (KV - 1) * S :]
            for k in range(KV - 2, -1, -1):
                s = jnp.where(row_kv == k, wide[:, k * S : (k + 1) * S], s)
            scores.append(s * SCALE)
        weights = []
        for (r, d, at), s in zip(rows, scores):
            b = batch_row(d, r % 2)
            keep = jnp.broadcast_to(mask_ref[pl.ds(b, 1), :], (T * H, S)) > 0
            m = jnp.max(jnp.where(keep, s, FAR_BELOW), axis=1, keepdims=True)
            e = jnp.where(keep, jnp.exp(s - m), 0.0)
            total = jnp.sum(e, axis=1, keepdims=True)
            exps[r] = e.reshape(T, H, S)
            weights.append(e)
            for t in range(T):
                here = lane == t * B + at
                part = slice(t * H, (t + 1) * H)
                block_peak = jnp.where(here, jnp.broadcast_to(m[part], (H, D)), block_peak)
                block_total = jnp.where(here, jnp.broadcast_to(total[part], (H, D)), block_total)
        for (r, _, _), e in zip(rows, weights):
            wide = jnp.concatenate(
                [jnp.where(row_kv == k, e, 0.0).astype(BF16) for k in range(KV)], axis=1
            )
            o = jnp.dot(wide, v_ref[r].reshape(KV * S, D), preferred_element_type=F32)
            sums[r] = o.reshape(T, H, D)
    peaks[...] = block_peak

    peak_tile, total_tile = block_peak, block_total
    for copy in small[1:]:
        copy.wait()
    for i in range(2):
        r = 2 * OUT.index(0) + i
        here = lane == t_own * B + 2 * SLOT[0] + i
        q = q_ref[t_own, r].astype(F32)
        ns = []
        for j in range(T):
            prod = q * expand_heads(nk_ref[j, i].astype(F32))
            sj = jnp.broadcast_to(jnp.sum(prod, axis=1, keepdims=True), (H, D)) * SCALE
            ns.append(jnp.where(j <= t_own, sj, FAR_BELOW))
        new_peak = ns[0]
        for j in range(1, T):
            new_peak = jnp.maximum(new_peak, ns[j])
        new_total, new_sum = zero, zero
        for j in range(T):
            ej = jnp.where(j <= t_own, jnp.exp(ns[j] - new_peak), 0.0)
            new_total = new_total + ej
            new_sum = new_sum + ej.astype(BF16).astype(F32) * expand_heads(nv_ref[j, i].astype(F32))
        old_peak = jnp.max(jnp.where(here, block_peak, -3e38), axis=1, keepdims=True)
        old_total = jnp.sum(jnp.where(here, block_total, 0.0), axis=1, keepdims=True)
        old_peak = jnp.broadcast_to(old_peak, (H, D))
        old_total = jnp.broadcast_to(old_total, (H, D))
        both = jnp.maximum(old_peak, new_peak)
        f_old = jnp.exp(old_peak - both)
        f_new = jnp.exp(new_peak - both)
        sums[r, t_own] = sums[r, t_own] * f_old + new_sum * f_new
        peak_tile = jnp.where(here, both, peak_tile)
        total_tile = jnp.where(here, old_total * f_old + new_total * f_new, total_tile)
    stat_own[0] = peak_tile
    stat_own[1] = total_tile

    pl.semaphore_wait(barrier, len(partners))
    for d in (2, 6):
        pl.semaphore_signal(ready, inc=1, device_id=z_dev(d), device_id_type=MESH)

    core_stat = remote(stat_own, stat_core, cs_s, cs_r, core_dev())
    core_copies = []
    for g, (first, count) in enumerate(CORE_GROUPS):
        rows = pl.ds(2 * first, 2 * count)
        core_copies.append(
            remote(
                sums.at[rows, pl.ds(NX * other, NX)], core_in.at[rows], cd_s.at[g], cd_r.at[g],
                core_dev(),
            )
        )
    core_stat.wait_recv()
    peak_c, total_c = stat_core[0], stat_core[1]
    pair_peak = jnp.maximum(peak_tile, peak_c)
    f_own = jnp.exp(peak_tile - pair_peak)
    f_core = jnp.exp(peak_c - pair_peak)
    pair_total = total_tile * f_own + total_c * f_core
    stat_pair[0] = pair_peak
    stat_pair[1] = pair_total

    x_stats = []
    for d in (2, 1, 3):
        x_stats.append(
            remote(stat_pair, stat_x.at[d - 1], xs_s.at[d - 1], xs_r.at[d - 1], x_dev(d))
        )
    fo = to_front(f_own, t_half * B)
    fc = to_front(f_core, t_half * B)
    for r, _, at in ROWS:
        for tl in range(NX):
            f_pair[0, tl, r] = lane_of(fo, tl * B + at)
            f_pair[1, tl, r] = lane_of(fc, tl * B + at)
    x_copies = []
    for g, (first, count) in enumerate(X_GROUPS):
        for h, (core_first, _) in enumerate(CORE_GROUPS):
            if first == core_first:
                core_copies[h].wait_recv()
        for tl in range(NX):
            for r in range(2 * first, 2 * (first + count)):
                pair[tl, r] = (
                    sums[r, t_half + tl] * f_pair[0, tl, r] + core_in[r, tl] * f_pair[1, tl, r]
                )
        rows = pl.ds(2 * first, 2 * count)
        x_copies.append(
            [
                remote(
                    pair.at[lax.rem(mx + d, NX), rows], x_in.at[d - 1, rows],
                    xd_s.at[g, d - 1], xd_r.at[g, d - 1], x_dev(d),
                )
                for d in (2, 1, 3)
            ]
        )
    for copy in x_stats:
        copy.wait_recv()
    group_peak = pair_peak
    for d in range(1, NX):
        group_peak = jnp.maximum(group_peak, stat_x[d - 1, 0])
    factors = [jnp.exp(pair_peak - group_peak)]
    group_total = pair_total * factors[0]
    for d in range(1, NX):
        f = jnp.exp(stat_x[d - 1, 0] - group_peak)
        factors.append(f)
        group_total = group_total + stat_x[d - 1, 1] * f

    shift = 2 * base
    in_row = lax.rem(lane, B)

    def by_row(tile):
        return jnp.where(
            in_row >= shift, pltpu.roll(tile, shift, 1), pltpu.roll(tile, lax.rem(shift + 112, 128), 1)
        )

    def by_slot(tile):
        return jnp.where(
            in_row < B - shift,
            pltpu.roll(tile, lax.rem(128 - shift, 128), 1),
            pltpu.roll(tile, lax.rem(144 - shift, 128), 1),
        )

    group_peak = by_row(group_peak)
    group_total = by_row(group_total)
    stat_group[0] = group_peak
    stat_group[1] = group_total
    pl.semaphore_wait(ready, 2)
    z_stats = [
        remote(stat_group, stat_z.at[d - 1], zs_s.at[d - 1], zs_r.at[d - 1], z_dev(d))
        for d in FAR_FIRST
    ]
    for d in range(NX):
        f = to_front(factors[d], t_own * B)
        for r, _, at in ROWS:
            f_x[d, r] = lane_of(f, at)
    z_copies = []
    for g, (first, count) in enumerate(X_GROUPS):
        for copy in x_copies[g]:
            copy.wait_recv()
        for m in range(first, first + count):
            d = OUT[m]
            for i in range(2):
                r = 2 * m + i
                acc = pair[mx, r] * f_x[0, r]
                for dx in range(1, NX):
                    acc = acc + x_in[dx - 1, r] * f_x[dx, r]
                z_out[m, i] = acc
            if d > 0:
                z_copies.append(
                    remote(z_out.at[m], z_in.at[d - 1], zd_s.at[d - 1], zd_r.at[d - 1], z_dev(d))
                )
    for copy in z_stats:
        copy.wait_recv()
    peak = group_peak
    for d in range(1, NZ):
        peak = jnp.maximum(peak, stat_z[d - 1, 0])
    factors = [jnp.exp(group_peak - peak)]
    total = group_total * factors[0]
    for d in range(1, NZ):
        f = jnp.exp(stat_z[d - 1, 0] - peak)
        factors.append(f)
        total = total + stat_z[d - 1, 1] * f
    inverse = 1.0 / total
    front = [to_front(f * inverse, t_own * B + b_own) for f in factors]
    scale = [[lane_of(f, i) for f in front] for i in range(2)]
    share = jnp.exp(peaks[...] - by_slot(peak)) * by_slot(inverse) * (CONTEXT / (T * HEADS_ALL))
    for copy in z_copies:
        copy.wait_recv()
    for i in range(2):
        acc = z_out[OUT.index(0), i] * scale[i][0]
        for d in range(1, NZ):
            acc = acc + z_in[d - 1, i] * scale[i][d]
        gathered[t_own, 2 * (base + SLOT[0]) + i] = acc

    own = gathered.at[t_own, pl.ds(2 * (base + SLOT[0]), 2)]
    gz = {}
    for d in FAR_FIRST:
        place = lax.rem(mz + d + NZ - 2, NZ) + SLOT[NZ - d]
        gz[d] = remote(
            own, gathered.at[t_own, pl.ds(2 * place, 2)], gz_s.at[d - 1], gz_r.at[d - 1], z_dev(d)
        )

    gx, gc = {}, []

    def span_of(t, first, count):
        return gathered.at[t, pl.ds(2 * (base + first), 2 * count)]

    def forward_x(g):
        first, count, arrivals = BACK_GROUPS[g]
        for d in arrivals:
            gz[d].wait_recv()
        span = span_of(t_own, first, count)
        for dx in (2, 1, 3):
            gx[g, dx] = remote(span, span, gx_s.at[g, dx - 1], gx_r.at[g, dx - 1], x_dev(dx))

    def forward_core(g, dx):
        span = span_of(t_half + lax.rem(mx + NX - dx, NX), *(NEAR, FAR)[g])
        gc.append(remote(span, span, gc_s.at[g, dx], gc_r.at[g, dx], core_dev()))

    forward_x(0)

    for r, d, at in ROWS:
        acc = exps[r, 0] * lane_of(share, at)
        for t in range(1, T):
            acc = acc + exps[r, t] * lane_of(share, t * B + at)
        b = batch_row(d, r % 2)
        imp_part[b // 4, pl.ds(lax.rem(b, 4), 1)] = jnp.sum(acc, axis=0, keepdims=True)
    y_copies = []
    for d in (2, 1, 3):
        y_copies.append(
            remote(
                imp_part.at[lax.rem(my + d, NY)], imp_in.at[d - 1], y_s.at[d - 1], y_r.at[d - 1],
                y_dev(d),
            )
        )

    forward_x(1)
    forward_x(2)
    forward_core(0, 0)
    forward_x(3)
    forward_core(1, 0)

    for copy in y_copies:
        copy.wait_recv()
    imp_ref[...] = imp_part[my] + imp_in[0] + imp_in[1] + imp_in[2]

    for dx in (1, 3, 2):
        for g in range(3):
            gx[g, dx].wait_recv()
        forward_core(0, dx)
    for dx in (1, 3, 2):
        gx[3, dx].wait_recv()
        forward_core(1, dx)

    wrapped = lax.broadcasted_iota(jnp.int32, (B, D), 0) < shift

    def emit(half):
        for tl in range(NX):
            t = NX * half + tl
            for h in range(H):
                straight = gathered[t, 0:B, h, :]
                beyond = gathered[t, B : 2 * B, h, :]
                out_ref[t, :, h * D : (h + 1) * D] = jnp.where(wrapped, beyond, straight).astype(BF16)

    emit(mc)
    for copy in gc:
        copy.wait_recv()
    emit(other)

    for copy in started:
        copy.wait_send()


def store(attended, importance, attended_out, importance_out, sem):
    copies = [
        pltpu.make_async_copy(attended, attended_out, sem.at[0]),
        pltpu.make_async_copy(importance, importance_out, sem.at[1]),
    ]
    for copy in copies:
        copy.start()
    for copy in copies:
        copy.wait()


def on_device(queries, cache_keys, stored_values, new_keys, decoded_values, keep_mask):
    any_space = pl.BlockSpec(memory_space=pl.ANY)
    vmem = pl.BlockSpec(memory_space=pltpu.VMEM)
    dma = pltpu.SemaphoreType.DMA
    attended, importance = pl.pallas_call(
        kernel,
        out_shape=(pltpu.VMEM((T, B, H * D), BF16), pltpu.VMEM((B // NY, S), F32)),
        in_specs=[any_space] * 6,
        out_specs=(vmem, vmem),
        scratch_shapes=[
            pltpu.VMEM((T, B, H, D), BF16),
            pltpu.VMEM((B, KV, S, D), BF16),
            pltpu.VMEM((B, KV, S, D), BF16),
            pltpu.VMEM((T, 2, KV, D), BF16),
            pltpu.VMEM((T, 2, KV, D), BF16),
            pltpu.VMEM((B, S), jnp.int32),
            pltpu.VMEM((B, T, H, D), F32),
            pltpu.VMEM((B, T, H, S), F32),
            pltpu.VMEM((H, D), F32),
            pltpu.VMEM((B, NX, H, D), F32),
            pltpu.VMEM((NX, B, H, D), F32),
            pltpu.VMEM((NX - 1, B, H, D), F32),
            pltpu.VMEM((NZ, 2, H, D), F32),
            pltpu.VMEM((NZ - 1, 2, H, D), F32),
            pltpu.VMEM((T, 2 * B, H, D), F32),
            pltpu.VMEM((NY, B // NY, S), F32),
            pltpu.VMEM((NY - 1, B // NY, S), F32),
            pltpu.VMEM((2, NX, B, H, D), F32),
            pltpu.VMEM((NX, B, H, D), F32),
            pltpu.VMEM((2, H, D), F32),
            pltpu.VMEM((2, H, D), F32),
            pltpu.VMEM((2, H, D), F32),
            pltpu.VMEM((NX - 1, 2, H, D), F32),
            pltpu.VMEM((2, H, D), F32),
            pltpu.VMEM((NZ - 1, 2, H, D), F32),
            dma((3,)),
            dma((3, NZ)),
            dma, dma, dma((2,)), dma((2,)),
            dma((NX - 1,)), dma((NX - 1,)), dma((4, NX - 1)), dma((4, NX - 1)),
            dma((NZ - 1,)), dma((NZ - 1,)), dma((NZ - 1,)), dma((NZ - 1,)),
            dma((NY - 1,)), dma((NY - 1,)),
            dma((NZ - 1,)), dma((NZ - 1,)), dma((4, NX - 1)), dma((4, NX - 1)),
            dma((2, NX)), dma((2, NX)),
            pltpu.SemaphoreType.REGULAR,
        ],
        compiler_params=pltpu.CompilerParams(
            collective_id=0, has_side_effects=True, vmem_limit_bytes=63 << 20
        ),
    )(queries, cache_keys, stored_values, new_keys, decoded_values, keep_mask)
    return pl.pallas_call(
        store,
        out_shape=(
            jax.ShapeDtypeStruct((T, B, H * D), BF16),
            jax.ShapeDtypeStruct((B // NY, S), F32),
        ),
        in_specs=[vmem, vmem],
        out_specs=(any_space, any_space),
        scratch_shapes=[dma((2,))],
    )(
        pltpu.with_memory_space_constraint(attended, pltpu.MemorySpace.VMEM),
        pltpu.with_memory_space_constraint(importance, pltpu.MemorySpace.VMEM),
    )


def solution(mesh):
    finer = Mesh(
        mesh.devices.reshape(mesh.shape["head"], NX, NZ, NC), ("head", "seq_0", "seq_1", "seq_2")
    )
    seq = ("seq_0", "seq_1", "seq_2")
    in_specs = (
        P(None, None, "head", None),
        P(None, "head", seq, None),
        P(None, "head", seq, None),
        P(None, None, "head", None),
        P(None, None, "head", None),
        P(None, seq),
    )
    out_specs = (P(None, None, "head"), P("head", seq))
    return jax.shard_map(
        on_device, mesh=finer, in_specs=in_specs, out_specs=out_specs, check_vma=False
    )
```

```python
import jax
import jax.numpy as jnp
from jax import lax
from jax.experimental import pallas as pl
from jax.experimental.pallas import tpu as pltpu
from jax.sharding import Mesh
from jax.sharding import PartitionSpec as P

F32 = jnp.float32
BF16 = jnp.bfloat16
MESH = pl.DeviceIdType.MESH
SCALE = 1.0 / 12.0
FAR_BELOW = -1e30

T, B, H, D = 8, 16, 8, 128
KV = 4
S = 128
NY, NX, NZ, NC = 4, 4, 8, 2
FAR_FIRST = (4, 3, 5, 2, 6, 1, 7)
OUT = FAR_FIRST + (0,)
SLOT = [(d + 2) % NZ for d in range(NZ)]
ROWS = [(2 * m + i, d, 2 * SLOT[d] + i) for m, d in enumerate(OUT) for i in range(2)]
FAR_ROWS = 2 * 3
NEAR_GROUPS = ((3, 2), (5, 2), (7, 1))
PEERS = [(dc, dx) for dc in range(NC) for dx in range(NX)]
SIBLING = PEERS.index((1, 0))
PEER_ORDER = (2, 6, 1, 3, 5, 7, 4)
FAR, NEAR = (5, 3), (0, 5)
BACK_GROUPS = ((2, 1, ()), (3, 2, (7, 6)), (0, 2, (1, 2)), (5, 3, (3, 5, 4)))
HEADS_ALL = 32
CONTEXT = S * NX * NZ * NC


def lane_of(tile, lane):
    return jnp.broadcast_to(tile[:, lane : lane + 1], (H, D))


def to_front(tile, lane):
    return pltpu.roll(tile, lax.rem(128 - lane, 128), 1)


def expand_heads(rows):
    sub = lax.broadcasted_iota(jnp.int32, (H, D), 0)
    out = jnp.broadcast_to(rows[KV - 1 : KV], (H, D))
    for k in range(KV - 2, -1, -1):
        out = jnp.where(sub < 2 * (k + 1), jnp.broadcast_to(rows[k : k + 1], (H, D)), out)
    return out


def kernel(
    q_hbm, k_hbm, v_hbm, nk_hbm, nv_hbm, mask_hbm,
    out_ref, imp_ref,
    q_ref, k_ref, v_ref, nk_ref, nv_ref, mask_ref,
    sums, exps, peaks, core_in, far_in, pair, x_in, z_out, z_in, gathered, imp_part, imp_in,
    f_pair, f_far, f_x, stat_own, stat_x, stat_group, stat_z,
    in_sem, chunk_sem,
    cd_s, cd_r, xs_s, xs_r, xf_s, xf_r, xd_s, xd_r, zs_s, zs_r, zd_s, zd_r, y_s, y_r,
    gz_s, gz_r, gx_s, gx_r, ge_s, ge_r, gc_s, gc_r, ready,
):
    my = lax.axis_index("head")
    mx = lax.axis_index("seq_0")
    mz = lax.axis_index("seq_1")
    mc = lax.axis_index("seq_2")
    other = 1 - mc
    t_half = NX * mc
    t_own = t_half + mx
    base = lax.rem(mz + NZ - 2, NZ)

    def core_dev():
        return {"seq_2": other}

    def peer_core(p):
        return other if PEERS[p][0] else mc

    def peer_dev(p):
        return {"seq_0": lax.rem(mx + PEERS[p][1], NX), "seq_2": peer_core(p)}

    def x_dev(d):
        return {"seq_0": lax.rem(mx + d, NX)}

    def z_dev(d):
        return {"seq_1": lax.rem(mz + d, NZ)}

    def y_dev(d):
        return {"head": lax.rem(my + d, NY)}

    started = []

    def remote(src, dst, ss, rs, dev):
        copy = pltpu.make_async_remote_copy(
            src_ref=src, dst_ref=dst, send_sem=ss, recv_sem=rs, device_id=dev, device_id_type=MESH
        )
        copy.start()
        started.append(copy)
        return copy

    def settle():
        for copy in started:
            copy.wait_send()
        started.clear()

    barrier = pltpu.get_barrier_semaphore()
    partners = (
        [z_dev(d) for d in (2, 6, 1, 7)]
        + [peer_dev(p) for p in PEER_ORDER[:-1]]
        + [y_dev(d) for d in (2, 1, 3)]
        + [core_dev()]
    )
    for dev in partners:
        pl.semaphore_signal(barrier, inc=1, device_id=dev, device_id_type=MESH)

    def chunk_loads(m):
        rows = pl.ds(2 * lax.rem(mz + OUT[m], NZ), 2)
        mine = pl.ds(2 * m, 2)
        return [
            pltpu.make_async_copy(q_hbm.at[:, rows], q_ref.at[:, mine], chunk_sem.at[0, m]),
            pltpu.make_async_copy(k_hbm.at[rows], k_ref.at[mine], chunk_sem.at[1, m]),
            pltpu.make_async_copy(v_hbm.at[rows], v_ref.at[mine], chunk_sem.at[2, m]),
        ]

    def batch_row(d, i):
        return 2 * lax.rem(mz + d, NZ) + i

    b_own = 2 * mz
    small = [
        pltpu.make_async_copy(mask_hbm, mask_ref, in_sem.at[0]),
        pltpu.make_async_copy(nk_hbm.at[:, pl.ds(b_own, 2)], nk_ref, in_sem.at[1]),
        pltpu.make_async_copy(nv_hbm.at[:, pl.ds(b_own, 2)], nv_ref, in_sem.at[2]),
    ]
    small[0].start()
    loads = [chunk_loads(m) for m in range(NZ)]
    for copies in loads:
        for copy in copies:
            copy.start()
    for copy in small[1:]:
        copy.start()
    small[0].wait()

    lane = lax.broadcasted_iota(jnp.int32, (H, D), 1)
    row_kv = lax.rem(lax.broadcasted_iota(jnp.int32, (T * H, S), 0), H) // 2

    zero = jnp.zeros((H, D), F32)
    block_peak, block_total = zero, zero
    for batch in (range(0, 4), range(4, 8)):
        for m in batch:
            for copy in loads[m]:
                copy.wait()
        rows = ROWS[2 * batch[0] : 2 * batch[-1] + 2]
        scores = []
        for r, _, _ in rows:
            q = q_ref[:, r].astype(F32).reshape(T * H, D).astype(BF16)
            wide = lax.dot_general(
                q, k_ref[r].reshape(KV * S, D), (((1,), (1,)), ((), ())), preferred_element_type=F32
            )
            s = wide[:, (KV - 1) * S :]
            for k in range(KV - 2, -1, -1):
                s = jnp.where(row_kv == k, wide[:, k * S : (k + 1) * S], s)
            scores.append(s * SCALE)
        weights = []
        for (r, d, at), s in zip(rows, scores):
            b = batch_row(d, r % 2)
            keep = jnp.broadcast_to(mask_ref[pl.ds(b, 1), :], (T * H, S)) > 0
            m = jnp.max(jnp.where(keep, s, FAR_BELOW), axis=1, keepdims=True)
            e = jnp.where(keep, jnp.exp(s - m), 0.0)
            total = jnp.sum(e, axis=1, keepdims=True)
            exps[r] = e.reshape(T, H, S)
            weights.append(e)
            for t in range(T):
                here = lane == t * B + at
                part = slice(t * H, (t + 1) * H)
                block_peak = jnp.where(here, jnp.broadcast_to(m[part], (H, D)), block_peak)
                block_total = jnp.where(here, jnp.broadcast_to(total[part], (H, D)), block_total)
        for (r, _, _), e in zip(rows, weights):
            wide = jnp.concatenate(
                [jnp.where(row_kv == k, e, 0.0).astype(BF16) for k in range(KV)], axis=1
            )
            o = jnp.dot(wide, v_ref[r].reshape(KV * S, D), preferred_element_type=F32)
            sums[r] = o.reshape(T, H, D)
    peaks[...] = block_peak

    peak_tile, total_tile = block_peak, block_total
    for copy in small[1:]:
        copy.wait()
    for i in range(2):
        r = 2 * OUT.index(0) + i
        here = lane == t_own * B + 2 * SLOT[0] + i
        q = q_ref[t_own, r].astype(F32)
        ns = []
        for j in range(T):
            prod = q * expand_heads(nk_ref[j, i].astype(F32))
            sj = jnp.broadcast_to(jnp.sum(prod, axis=1, keepdims=True), (H, D)) * SCALE
            ns.append(jnp.where(j <= t_own, sj, FAR_BELOW))
        new_peak = ns[0]
        for j in range(1, T):
            new_peak = jnp.maximum(new_peak, ns[j])
        new_total, new_sum = zero, zero
        for j in range(T):
            ej = jnp.where(j <= t_own, jnp.exp(ns[j] - new_peak), 0.0)
            new_total = new_total + ej
            new_sum = new_sum + ej.astype(BF16).astype(F32) * expand_heads(nv_ref[j, i].astype(F32))
        old_peak = jnp.max(jnp.where(here, block_peak, -3e38), axis=1, keepdims=True)
        old_total = jnp.sum(jnp.where(here, block_total, 0.0), axis=1, keepdims=True)
        old_peak = jnp.broadcast_to(old_peak, (H, D))
        old_total = jnp.broadcast_to(old_total, (H, D))
        both = jnp.maximum(old_peak, new_peak)
        f_old = jnp.exp(old_peak - both)
        f_new = jnp.exp(new_peak - both)
        sums[r, t_own] = sums[r, t_own] * f_old + new_sum * f_new
        peak_tile = jnp.where(here, both, peak_tile)
        total_tile = jnp.where(here, old_total * f_old + new_total * f_new, total_tile)
    stat_own[0] = peak_tile
    stat_own[1] = total_tile

    pl.semaphore_wait(barrier, len(partners))
    for d in (2, 6):
        pl.semaphore_signal(ready, inc=1, device_id=z_dev(d), device_id_type=MESH)

    stats = [
        remote(stat_own, stat_x.at[p - 1], xs_s.at[p - 1], xs_r.at[p - 1], peer_dev(p))
        for p in PEER_ORDER
    ]
    far_rows = pl.ds(0, FAR_ROWS)
    far_copies = [
        remote(
            sums.at[far_rows, NX * peer_core(p) + lax.rem(mx + PEERS[p][1], NX)],
            far_in.at[p - 1], xf_s.at[p - 1], xf_r.at[p - 1], peer_dev(p),
        )
        for p in PEER_ORDER
    ]

    near_rows = pl.ds(FAR_ROWS, B - FAR_ROWS)
    core_copy = remote(
        sums.at[near_rows, pl.ds(NX * other, NX)], core_in.at[near_rows], cd_s, cd_r, core_dev()
    )
    stats[PEER_ORDER.index(SIBLING)].wait_recv()
    peak_c = stat_x[SIBLING - 1, 0]
    pair_peak = jnp.maximum(peak_tile, peak_c)
    fo = to_front(jnp.exp(peak_tile - pair_peak), t_half * B)
    fc = to_front(jnp.exp(peak_c - pair_peak), t_half * B)
    for r, _, at in ROWS[FAR_ROWS:]:
        for tl in range(NX):
            f_pair[0, tl, r] = lane_of(fo, tl * B + at)
            f_pair[1, tl, r] = lane_of(fc, tl * B + at)

    core_copy.wait_recv()
    x_copies = []
    for g, (first, count) in enumerate(NEAR_GROUPS):
        for tl in range(NX):
            for r in range(2 * first, 2 * (first + count)):
                pair[tl, r] = (
                    sums[r, t_half + tl] * f_pair[0, tl, r] + core_in[r, tl] * f_pair[1, tl, r]
                )
        rows = pl.ds(2 * first, 2 * count)
        x_copies.append(
            [
                remote(
                    pair.at[lax.rem(mx + d, NX), rows], x_in.at[d - 1, rows],
                    xd_s.at[g, d - 1], xd_r.at[g, d - 1], x_dev(d),
                )
                for d in (2, 1, 3)
            ]
        )
    for p, copy in zip(PEER_ORDER, stats):
        if p != SIBLING:
            copy.wait_recv()
    peer_peak = [peak_tile] + [stat_x[p - 1, 0] for p in range(1, len(PEERS))]
    group_peak = peak_tile
    for p in range(1, len(PEERS)):
        group_peak = jnp.maximum(group_peak, peer_peak[p])
    factors = [jnp.exp(one - group_peak) for one in peer_peak]
    group_total = total_tile * factors[0]
    for p in range(1, len(PEERS)):
        group_total = group_total + stat_x[p - 1, 1] * factors[p]

    shift = 2 * base
    in_row = lax.rem(lane, B)

    def by_row(tile):
        return jnp.where(
            in_row >= shift, pltpu.roll(tile, shift, 1), pltpu.roll(tile, lax.rem(shift + 112, 128), 1)
        )

    def by_slot(tile):
        return jnp.where(
            in_row < B - shift,
            pltpu.roll(tile, lax.rem(128 - shift, 128), 1),
            pltpu.roll(tile, lax.rem(144 - shift, 128), 1),
        )

    group_peak = by_row(group_peak)
    group_total = by_row(group_total)
    stat_group[0] = group_peak
    stat_group[1] = group_total
    pl.semaphore_wait(ready, 2)
    z_stats = [
        remote(stat_group, stat_z.at[d - 1], zs_s.at[d - 1], zs_r.at[d - 1], z_dev(d))
        for d in FAR_FIRST
    ]
    for p in range(len(PEERS)):
        f = to_front(factors[p], t_own * B)
        for r, _, at in ROWS[:FAR_ROWS]:
            f_far[p, r] = lane_of(f, at)
    for dx in range(NX):
        f = to_front(jnp.maximum(factors[dx], factors[NX + dx]), t_own * B)
        for r, _, at in ROWS[FAR_ROWS:]:
            f_x[dx, r] = lane_of(f, at)
    z_copies = []

    def send_z(m):
        d = OUT[m]
        if d > 0:
            z_copies.append(
                remote(z_out.at[m], z_in.at[d - 1], zd_s.at[d - 1], zd_r.at[d - 1], z_dev(d))
            )

    for copy in far_copies:
        copy.wait_recv()
    for m in range(FAR_ROWS // 2):
        for i in range(2):
            r = 2 * m + i
            acc = sums[r, t_own] * f_far[0, r]
            for p in range(1, len(PEERS)):
                acc = acc + far_in[p - 1, r] * f_far[p, r]
            z_out[m, i] = acc
        send_z(m)
    for g, (first, count) in enumerate(NEAR_GROUPS):
        for copy in x_copies[g]:
            copy.wait_recv()
        for m in range(first, first + count):
            for i in range(2):
                r = 2 * m + i
                acc = pair[mx, r] * f_x[0, r]
                for dx in range(1, NX):
                    acc = acc + x_in[dx - 1, r] * f_x[dx, r]
                z_out[m, i] = acc
            send_z(m)
    for copy in z_stats:
        copy.wait_recv()
    peak = group_peak
    for d in range(1, NZ):
        peak = jnp.maximum(peak, stat_z[d - 1, 0])
    factors = [jnp.exp(group_peak - peak)]
    total = group_total * factors[0]
    for d in range(1, NZ):
        f = jnp.exp(stat_z[d - 1, 0] - peak)
        factors.append(f)
        total = total + stat_z[d - 1, 1] * f
    inverse = 1.0 / total
    front = [to_front(f * inverse, t_own * B + b_own) for f in factors]
    scale = [[lane_of(f, i) for f in front] for i in range(2)]
    share = jnp.exp(peaks[...] - by_slot(peak)) * by_slot(inverse) * (CONTEXT / (T * HEADS_ALL))
    for copy in z_copies:
        copy.wait_recv()
    for i in range(2):
        acc = z_out[OUT.index(0), i] * scale[i][0]
        for d in range(1, NZ):
            acc = acc + z_in[d - 1, i] * scale[i][d]
        gathered[t_own, 2 * (base + SLOT[0]) + i] = acc

    own = gathered.at[t_own, pl.ds(2 * (base + SLOT[0]), 2)]
    gz = {}
    for d in FAR_FIRST:
        place = lax.rem(mz + d + NZ - 2, NZ) + SLOT[NZ - d]
        gz[d] = remote(
            own, gathered.at[t_own, pl.ds(2 * place, 2)], gz_s.at[d - 1], gz_r.at[d - 1], z_dev(d)
        )

    gx, ge, gc = {}, {}, []

    def span_of(t, first, count):
        return gathered.at[t, pl.ds(2 * (base + first), 2 * count)]

    def forward_x(g):
        first, count, arrivals = BACK_GROUPS[g]
        for d in arrivals:
            gz[d].wait_recv()
        span = span_of(t_own, first, count)
        for dx in (2, 1, 3):
            gx[g, dx] = remote(span, span, gx_s.at[g, dx - 1], gx_r.at[g, dx - 1], x_dev(dx))
            if g == 3:
                ge[dx] = remote(
                    span, span, ge_s.at[dx - 1], ge_r.at[dx - 1], peer_dev(NX + dx)
                )

    def forward_core(g, dx):
        span = span_of(t_half + lax.rem(mx + NX - dx, NX), *(NEAR, FAR)[g])
        gc.append(remote(span, span, gc_s.at[g, dx], gc_r.at[g, dx], core_dev()))

    forward_x(0)

    for r, d, at in ROWS:
        acc = exps[r, 0] * lane_of(share, at)
        for t in range(1, T):
            acc = acc + exps[r, t] * lane_of(share, t * B + at)
        b = batch_row(d, r % 2)
        imp_part[b // 4, pl.ds(lax.rem(b, 4), 1)] = jnp.sum(acc, axis=0, keepdims=True)
    y_copies = []
    for d in (2, 1, 3):
        y_copies.append(
            remote(
                imp_part.at[lax.rem(my + d, NY)], imp_in.at[d - 1], y_s.at[d - 1], y_r.at[d - 1],
                y_dev(d),
            )
        )

    settle()

    forward_x(1)
    forward_x(2)
    forward_core(0, 0)
    forward_x(3)
    forward_core(1, 0)

    for copy in y_copies:
        copy.wait_recv()
    imp_ref[...] = imp_part[my] + imp_in[0] + imp_in[1] + imp_in[2]

    settle()

    for dx in (1, 3, 2):
        for g in range(3):
            gx[g, dx].wait_recv()
        forward_core(0, dx)
    for dx in (1, 3, 2):
        gx[3, dx].wait_recv()

    wrapped = lax.broadcasted_iota(jnp.int32, (B, D), 0) < shift

    def emit(half):
        for tl in range(NX):
            t = NX * half + tl
            for h in range(H):
                straight = gathered[t, 0:B, h, :]
                beyond = gathered[t, B : 2 * B, h, :]
                out_ref[t, :, h * D : (h + 1) * D] = jnp.where(wrapped, beyond, straight).astype(BF16)

    emit(mc)
    for copy in gc + list(ge.values()):
        copy.wait_recv()
    emit(other)

    settle()


def store(attended, importance, attended_out, importance_out, sem):
    copies = [
        pltpu.make_async_copy(attended, attended_out, sem.at[0]),
        pltpu.make_async_copy(importance, importance_out, sem.at[1]),
    ]
    for copy in copies:
        copy.start()
    for copy in copies:
        copy.wait()


def on_device(queries, cache_keys, stored_values, new_keys, decoded_values, keep_mask):
    any_space = pl.BlockSpec(memory_space=pl.ANY)
    vmem = pl.BlockSpec(memory_space=pltpu.VMEM)
    dma = pltpu.SemaphoreType.DMA
    attended, importance = pl.pallas_call(
        kernel,
        out_shape=(pltpu.VMEM((T, B, H * D), BF16), pltpu.VMEM((B // NY, S), F32)),
        in_specs=[any_space] * 6,
        out_specs=(vmem, vmem),
        scratch_shapes=[
            pltpu.VMEM((T, B, H, D), BF16),
            pltpu.VMEM((B, KV, S, D), BF16),
            pltpu.VMEM((B, KV, S, D), BF16),
            pltpu.VMEM((T, 2, KV, D), BF16),
            pltpu.VMEM((T, 2, KV, D), BF16),
            pltpu.VMEM((B, S), jnp.int32),
            pltpu.VMEM((B, T, H, D), F32),
            pltpu.VMEM((B, T, H, S), F32),
            pltpu.VMEM((H, D), F32),
            pltpu.VMEM((B, NX, H, D), F32),
            pltpu.VMEM((len(PEERS) - 1, FAR_ROWS, H, D), F32),
            pltpu.VMEM((NX, B, H, D), F32),
            pltpu.VMEM((NX - 1, B, H, D), F32),
            pltpu.VMEM((NZ, 2, H, D), F32),
            pltpu.VMEM((NZ - 1, 2, H, D), F32),
            pltpu.VMEM((T, 2 * B, H, D), F32),
            pltpu.VMEM((NY, B // NY, S), F32),
            pltpu.VMEM((NY - 1, B // NY, S), F32),
            pltpu.VMEM((2, NX, B, H, D), F32),
            pltpu.VMEM((len(PEERS), FAR_ROWS, H, D), F32),
            pltpu.VMEM((NX, B, H, D), F32),
            pltpu.VMEM((2, H, D), F32),
            pltpu.VMEM((len(PEERS) - 1, 2, H, D), F32),
            pltpu.VMEM((2, H, D), F32),
            pltpu.VMEM((NZ - 1, 2, H, D), F32),
            dma((3,)),
            dma((3, NZ)),
            dma, dma, dma((len(PEERS) - 1,)), dma((len(PEERS) - 1,)),
            dma((len(PEERS) - 1,)), dma((len(PEERS) - 1,)), dma((3, NX - 1)), dma((3, NX - 1)),
            dma((NZ - 1,)), dma((NZ - 1,)), dma((NZ - 1,)), dma((NZ - 1,)),
            dma((NY - 1,)), dma((NY - 1,)),
            dma((NZ - 1,)), dma((NZ - 1,)), dma((4, NX - 1)), dma((4, NX - 1)),
            dma((NX - 1,)), dma((NX - 1,)), dma((2, NX)), dma((2, NX)),
            pltpu.SemaphoreType.REGULAR,
        ],
        compiler_params=pltpu.CompilerParams(
            collective_id=0, has_side_effects=True, vmem_limit_bytes=63 << 20
        ),
    )(queries, cache_keys, stored_values, new_keys, decoded_values, keep_mask)
    return pl.pallas_call(
        store,
        out_shape=(
            jax.ShapeDtypeStruct((T, B, H * D), BF16),
            jax.ShapeDtypeStruct((B // NY, S), F32),
        ),
        in_specs=[vmem, vmem],
        out_specs=(any_space, any_space),
        scratch_shapes=[dma((2,))],
    )(
        pltpu.with_memory_space_constraint(attended, pltpu.MemorySpace.VMEM),
        pltpu.with_memory_space_constraint(importance, pltpu.MemorySpace.VMEM),
    )


def solution(mesh):
    finer = Mesh(
        mesh.devices.reshape(mesh.shape["head"], NX, NZ, NC), ("head", "seq_0", "seq_1", "seq_2")
    )
    seq = ("seq_0", "seq_1", "seq_2")
    in_specs = (
        P(None, None, "head", None),
        P(None, "head", seq, None),
        P(None, "head", seq, None),
        P(None, None, "head", None),
        P(None, None, "head", None),
        P(None, seq),
    )
    out_specs = (P(None, None, "head"), P("head", seq))
    return jax.shard_map(
        on_device, mesh=finer, in_specs=in_specs, out_specs=out_specs, check_vma=False
    )
```

```python
import jax
import jax.numpy as jnp
from jax import lax
from jax.experimental import pallas as pl
from jax.experimental.pallas import tpu as pltpu
from jax.sharding import Mesh
from jax.sharding import PartitionSpec as P

F32 = jnp.float32
BF16 = jnp.bfloat16
MESH = pl.DeviceIdType.MESH
SCALE = 1.0 / 12.0
FAR_BELOW = -1e30

T, B, H, D = 8, 16, 8, 128
KV = 4
S = 128
NY, NX, NZ, NC = 4, 4, 8, 2
FAR_FIRST = (4, 3, 5, 2, 6, 1, 7)
OUT = FAR_FIRST + (0,)
SLOT = [(d + 2) % NZ for d in range(NZ)]
ROWS = [(2 * m + i, d, 2 * SLOT[d] + i) for m, d in enumerate(OUT) for i in range(2)]
FAR_ROWS = 2 * 3
NEAR_GROUPS = ((3, 2), (5, 2), (7, 1))
PEERS = [(dc, dx) for dc in range(NC) for dx in range(NX)]
SIBLING = PEERS.index((1, 0))
PEER_ORDER = (2, 6, 1, 3, 5, 7, 4)
FAR, NEAR = (5, 3), (0, 5)
BACK_GROUPS = ((2, 1, ()), (3, 2, (7, 6)), (0, 2, (1, 2)), (5, 3, (3, 5, 4)))
HEADS_ALL = 32
CONTEXT = S * NX * NZ * NC


def lane_of(tile, lane):
    return jnp.broadcast_to(tile[:, lane : lane + 1], (H, D))


def to_front(tile, lane):
    return pltpu.roll(tile, lax.rem(128 - lane, 128), 1)


def expand_heads(rows):
    sub = lax.broadcasted_iota(jnp.int32, (H, D), 0)
    out = jnp.broadcast_to(rows[KV - 1 : KV], (H, D))
    for k in range(KV - 2, -1, -1):
        out = jnp.where(sub < 2 * (k + 1), jnp.broadcast_to(rows[k : k + 1], (H, D)), out)
    return out


def kernel(
    q_hbm, k_hbm, v_hbm, nk_hbm, nv_hbm, mask_hbm,
    out_ref, imp_ref,
    q_ref, k_ref, v_ref, nk_ref, nv_ref, mask_ref,
    sums, exps, peaks, core_in, far_in, pair, x_in, z_out, z_in, gathered, imp_part, imp_in,
    f_pair, f_far, f_x, stat_own, stat_x, stat_group, stat_z, stat_full,
    in_sem, chunk_sem,
    cd_s, cd_r, xs_s, xs_r, xf_s, xf_r, xd_s, xd_r, zs_s, zs_r, zd_s, zd_r, y_s, y_r,
    gz_s, gz_r, gx_s, gx_r, ge_s, ge_r, gc_s, gc_r, hs_s, hs_r, ready,
):
    my = lax.axis_index("head")
    mx = lax.axis_index("seq_0")
    mz = lax.axis_index("seq_1")
    mc = lax.axis_index("seq_2")
    other = 1 - mc
    t_half = NX * mc
    t_own = t_half + mx
    base = lax.rem(mz + NZ - 2, NZ)

    def core_dev():
        return {"seq_2": other}

    def peer_core(p):
        return other if PEERS[p][0] else mc

    def peer_dev(p):
        return {"seq_0": lax.rem(mx + PEERS[p][1], NX), "seq_2": peer_core(p)}

    def x_dev(d):
        return {"seq_0": lax.rem(mx + d, NX)}

    def z_dev(d):
        return {"seq_1": lax.rem(mz + d, NZ)}

    def y_dev(d):
        return {"head": lax.rem(my + d, NY)}

    started = []

    def remote(src, dst, ss, rs, dev):
        copy = pltpu.make_async_remote_copy(
            src_ref=src, dst_ref=dst, send_sem=ss, recv_sem=rs, device_id=dev, device_id_type=MESH
        )
        copy.start()
        started.append(copy)
        return copy

    def settle():
        for copy in started:
            copy.wait_send()
        started.clear()

    barrier = pltpu.get_barrier_semaphore()
    partners = (
        [z_dev(d) for d in (2, 6, 1, 7)]
        + [peer_dev(p) for p in PEER_ORDER[:-1]]
        + [y_dev(d) for d in (2, 1, 3)]
        + [core_dev()]
    )
    for dev in partners:
        pl.semaphore_signal(barrier, inc=1, device_id=dev, device_id_type=MESH)

    def chunk_loads(m):
        rows = pl.ds(2 * lax.rem(mz + OUT[m], NZ), 2)
        mine = pl.ds(2 * m, 2)
        return [
            pltpu.make_async_copy(q_hbm.at[:, rows], q_ref.at[:, mine], chunk_sem.at[0, m]),
            pltpu.make_async_copy(k_hbm.at[rows], k_ref.at[mine], chunk_sem.at[1, m]),
            pltpu.make_async_copy(v_hbm.at[rows], v_ref.at[mine], chunk_sem.at[2, m]),
        ]

    def batch_row(d, i):
        return 2 * lax.rem(mz + d, NZ) + i

    b_own = 2 * mz
    small = [
        pltpu.make_async_copy(mask_hbm, mask_ref, in_sem.at[0]),
        pltpu.make_async_copy(nk_hbm.at[:, pl.ds(b_own, 2)], nk_ref, in_sem.at[1]),
        pltpu.make_async_copy(nv_hbm.at[:, pl.ds(b_own, 2)], nv_ref, in_sem.at[2]),
    ]
    small[0].start()
    loads = [chunk_loads(m) for m in range(NZ)]
    for copies in loads:
        for copy in copies:
            copy.start()
    for copy in small[1:]:
        copy.start()
    small[0].wait()

    lane = lax.broadcasted_iota(jnp.int32, (H, D), 1)
    row_kv = lax.rem(lax.broadcasted_iota(jnp.int32, (T * H, S), 0), H) // 2

    zero = jnp.zeros((H, D), F32)
    block_peak, block_total = zero, zero
    for batch in (range(0, 4), range(4, 8)):
        for m in batch:
            for copy in loads[m]:
                copy.wait()
        rows = ROWS[2 * batch[0] : 2 * batch[-1] + 2]
        scores = []
        for r, _, _ in rows:
            q = q_ref[:, r].astype(F32).reshape(T * H, D).astype(BF16)
            wide = lax.dot_general(
                q, k_ref[r].reshape(KV * S, D), (((1,), (1,)), ((), ())), preferred_element_type=F32
            )
            s = wide[:, (KV - 1) * S :]
            for k in range(KV - 2, -1, -1):
                s = jnp.where(row_kv == k, wide[:, k * S : (k + 1) * S], s)
            scores.append(s * SCALE)
        weights = []
        for (r, d, at), s in zip(rows, scores):
            b = batch_row(d, r % 2)
            keep = jnp.broadcast_to(mask_ref[pl.ds(b, 1), :], (T * H, S)) > 0
            m = jnp.max(jnp.where(keep, s, FAR_BELOW), axis=1, keepdims=True)
            e = jnp.where(keep, jnp.exp(s - m), 0.0)
            total = jnp.sum(e, axis=1, keepdims=True)
            exps[r] = e.reshape(T, H, S)
            weights.append(e)
            for t in range(T):
                here = lane == t * B + at
                part = slice(t * H, (t + 1) * H)
                block_peak = jnp.where(here, jnp.broadcast_to(m[part], (H, D)), block_peak)
                block_total = jnp.where(here, jnp.broadcast_to(total[part], (H, D)), block_total)
        for (r, _, _), e in zip(rows, weights):
            wide = jnp.concatenate(
                [jnp.where(row_kv == k, e, 0.0).astype(BF16) for k in range(KV)], axis=1
            )
            o = jnp.dot(wide, v_ref[r].reshape(KV * S, D), preferred_element_type=F32)
            sums[r] = o.reshape(T, H, D)
    peaks[...] = block_peak

    peak_tile, total_tile = block_peak, block_total
    for copy in small[1:]:
        copy.wait()
    for i in range(2):
        r = 2 * OUT.index(0) + i
        here = lane == t_own * B + 2 * SLOT[0] + i
        q = q_ref[t_own, r].astype(F32)
        ns = []
        for j in range(T):
            prod = q * expand_heads(nk_ref[j, i].astype(F32))
            sj = jnp.broadcast_to(jnp.sum(prod, axis=1, keepdims=True), (H, D)) * SCALE
            ns.append(jnp.where(j <= t_own, sj, FAR_BELOW))
        new_peak = ns[0]
        for j in range(1, T):
            new_peak = jnp.maximum(new_peak, ns[j])
        new_total, new_sum = zero, zero
        for j in range(T):
            ej = jnp.where(j <= t_own, jnp.exp(ns[j] - new_peak), 0.0)
            new_total = new_total + ej
            new_sum = new_sum + ej.astype(BF16).astype(F32) * expand_heads(nv_ref[j, i].astype(F32))
        old_peak = jnp.max(jnp.where(here, block_peak, -3e38), axis=1, keepdims=True)
        old_total = jnp.sum(jnp.where(here, block_total, 0.0), axis=1, keepdims=True)
        old_peak = jnp.broadcast_to(old_peak, (H, D))
        old_total = jnp.broadcast_to(old_total, (H, D))
        both = jnp.maximum(old_peak, new_peak)
        f_old = jnp.exp(old_peak - both)
        f_new = jnp.exp(new_peak - both)
        sums[r, t_own] = sums[r, t_own] * f_old + new_sum * f_new
        peak_tile = jnp.where(here, both, peak_tile)
        total_tile = jnp.where(here, old_total * f_old + new_total * f_new, total_tile)
    low = lane < D // 2

    def swap(tile):
        return pltpu.roll(tile, D // 2, 1)

    stat_own[0] = jnp.where(low, peak_tile, swap(total_tile))
    stat_own[1] = jnp.where(low, swap(peak_tile), total_tile)
    mine = stat_own[mc]

    pl.semaphore_wait(barrier, len(partners))
    for d in (2, 6):
        pl.semaphore_signal(ready, inc=1, device_id=z_dev(d), device_id_type=MESH)

    stats = [
        remote(stat_own.at[peer_core(p)], stat_x.at[p - 1], xs_s.at[p - 1], xs_r.at[p - 1], peer_dev(p))
        for p in PEER_ORDER
    ]
    far_rows = pl.ds(0, FAR_ROWS)
    far_copies = [
        remote(
            sums.at[far_rows, NX * peer_core(p) + lax.rem(mx + PEERS[p][1], NX)],
            far_in.at[p - 1], xf_s.at[p - 1], xf_r.at[p - 1], peer_dev(p),
        )
        for p in PEER_ORDER
    ]

    near_rows = pl.ds(FAR_ROWS, B - FAR_ROWS)
    core_copy = remote(
        sums.at[near_rows, pl.ds(NX * other, NX)], core_in.at[near_rows], cd_s, cd_r, core_dev()
    )
    stats[PEER_ORDER.index(SIBLING)].wait_recv()
    peak_c = stat_x[SIBLING - 1]
    pair_peak = jnp.maximum(mine, peak_c)
    fo = jnp.exp(mine - pair_peak)
    fc = jnp.exp(peak_c - pair_peak)
    for r, _, at in ROWS[FAR_ROWS:]:
        for tl in range(NX):
            f_pair[0, tl, r] = lane_of(fo, tl * B + at)
            f_pair[1, tl, r] = lane_of(fc, tl * B + at)

    core_copy.wait_recv()
    x_copies = []
    for g, (first, count) in enumerate(NEAR_GROUPS):
        for tl in range(NX):
            for r in range(2 * first, 2 * (first + count)):
                pair[tl, r] = (
                    sums[r, t_half + tl] * f_pair[0, tl, r] + core_in[r, tl] * f_pair[1, tl, r]
                )
        rows = pl.ds(2 * first, 2 * count)
        x_copies.append(
            [
                remote(
                    pair.at[lax.rem(mx + d, NX), rows], x_in.at[d - 1, rows],
                    xd_s.at[g, d - 1], xd_r.at[g, d - 1], x_dev(d),
                )
                for d in (2, 1, 3)
            ]
        )
    for p, copy in zip(PEER_ORDER, stats):
        if p != SIBLING:
            copy.wait_recv()
    peer_peak = [mine] + [stat_x[p - 1] for p in range(1, len(PEERS))]
    group_peak = mine
    for p in range(1, len(PEERS)):
        group_peak = jnp.maximum(group_peak, peer_peak[p])
    factors = [jnp.exp(one - group_peak) for one in peer_peak]
    group_total = swap(mine) * factors[0]
    for p in range(1, len(PEERS)):
        group_total = group_total + swap(peer_peak[p]) * factors[p]

    shift = 2 * base
    in_row = lax.rem(lane, B)

    def by_row(tile):
        return jnp.where(
            in_row >= shift, pltpu.roll(tile, shift, 1), pltpu.roll(tile, lax.rem(shift + 112, 128), 1)
        )

    def by_slot(tile):
        return jnp.where(
            in_row < B - shift,
            pltpu.roll(tile, lax.rem(128 - shift, 128), 1),
            pltpu.roll(tile, lax.rem(144 - shift, 128), 1),
        )

    group_peak = by_row(group_peak)
    group_total = by_row(group_total)
    stat_group[...] = jnp.where(low, group_peak, swap(group_total))
    pl.semaphore_wait(ready, 2)
    z_stats = [
        remote(stat_group, stat_z.at[d - 1], zs_s.at[d - 1], zs_r.at[d - 1], z_dev(d))
        for d in FAR_FIRST
    ]
    for p in range(len(PEERS)):
        f = to_front(factors[p], mx * B)
        for r, _, at in ROWS[:FAR_ROWS]:
            f_far[p, r] = lane_of(f, at)
    for dx in range(NX):
        f = to_front(jnp.maximum(factors[dx], factors[NX + dx]), mx * B)
        for r, _, at in ROWS[FAR_ROWS:]:
            f_x[dx, r] = lane_of(f, at)
    z_copies = []

    def send_z(m):
        d = OUT[m]
        if d > 0:
            z_copies.append(
                remote(z_out.at[m], z_in.at[d - 1], zd_s.at[d - 1], zd_r.at[d - 1], z_dev(d))
            )

    for copy in far_copies:
        copy.wait_recv()
    for m in range(FAR_ROWS // 2):
        for i in range(2):
            r = 2 * m + i
            acc = sums[r, t_own] * f_far[0, r]
            for p in range(1, len(PEERS)):
                acc = acc + far_in[p - 1, r] * f_far[p, r]
            z_out[m, i] = acc
        send_z(m)
    for g, (first, count) in enumerate(NEAR_GROUPS):
        for copy in x_copies[g]:
            copy.wait_recv()
        for m in range(first, first + count):
            for i in range(2):
                r = 2 * m + i
                acc = pair[mx, r] * f_x[0, r]
                for dx in range(1, NX):
                    acc = acc + x_in[dx - 1, r] * f_x[dx, r]
                z_out[m, i] = acc
            send_z(m)
    for copy in z_stats:
        copy.wait_recv()
    peak = group_peak
    for d in range(1, NZ):
        peak = jnp.maximum(peak, stat_z[d - 1])
    factors = [jnp.exp(group_peak - peak)]
    total = group_total * factors[0]
    for d in range(1, NZ):
        f = jnp.exp(stat_z[d - 1] - peak)
        factors.append(f)
        total = total + swap(stat_z[d - 1]) * f
    inverse = 1.0 / total
    front = [to_front(f * inverse, mx * B + b_own) for f in factors]
    scale = [[lane_of(f, i) for f in front] for i in range(2)]
    stat_full[mc] = jnp.where(low, peak, swap(total))
    half_stat = remote(stat_full.at[mc], stat_full.at[mc], hs_s, hs_r, core_dev())
    for copy in z_copies:
        copy.wait_recv()
    for i in range(2):
        acc = z_out[OUT.index(0), i] * scale[i][0]
        for d in range(1, NZ):
            acc = acc + z_in[d - 1, i] * scale[i][d]
        gathered[t_own, 2 * (base + SLOT[0]) + i] = acc

    own = gathered.at[t_own, pl.ds(2 * (base + SLOT[0]), 2)]
    gz = {}
    for d in FAR_FIRST:
        place = lax.rem(mz + d + NZ - 2, NZ) + SLOT[NZ - d]
        gz[d] = remote(
            own, gathered.at[t_own, pl.ds(2 * place, 2)], gz_s.at[d - 1], gz_r.at[d - 1], z_dev(d)
        )

    gx, ge, gc = {}, {}, []

    def span_of(t, first, count):
        return gathered.at[t, pl.ds(2 * (base + first), 2 * count)]

    def forward_x(g):
        first, count, arrivals = BACK_GROUPS[g]
        for d in arrivals:
            gz[d].wait_recv()
        span = span_of(t_own, first, count)
        for dx in (2, 1, 3):
            gx[g, dx] = remote(span, span, gx_s.at[g, dx - 1], gx_r.at[g, dx - 1], x_dev(dx))
            if g == 3:
                ge[dx] = remote(
                    span, span, ge_s.at[dx - 1], ge_r.at[dx - 1], peer_dev(NX + dx)
                )

    def forward_core(g, dx):
        span = span_of(t_half + lax.rem(mx + NX - dx, NX), *(NEAR, FAR)[g])
        gc.append(remote(span, span, gc_s.at[g, dx], gc_r.at[g, dx], core_dev()))

    forward_x(0)

    half_stat.wait_recv()
    full_peak = by_slot(jnp.where(low, stat_full[0], swap(stat_full[1])))
    full_total = by_slot(jnp.where(low, swap(stat_full[0]), stat_full[1]))
    share = jnp.exp(peaks[...] - full_peak) / full_total * (CONTEXT / (T * HEADS_ALL))
    for r, d, at in ROWS:
        acc = exps[r, 0] * lane_of(share, at)
        for t in range(1, T):
            acc = acc + exps[r, t] * lane_of(share, t * B + at)
        b = batch_row(d, r % 2)
        imp_part[b // 4, pl.ds(lax.rem(b, 4), 1)] = jnp.sum(acc, axis=0, keepdims=True)
    y_copies = []
    for d in (2, 1, 3):
        y_copies.append(
            remote(
                imp_part.at[lax.rem(my + d, NY)], imp_in.at[d - 1], y_s.at[d - 1], y_r.at[d - 1],
                y_dev(d),
            )
        )

    settle()

    forward_x(1)
    forward_x(2)
    forward_core(0, 0)
    forward_x(3)
    forward_core(1, 0)

    for copy in y_copies:
        copy.wait_recv()
    imp_ref[...] = imp_part[my] + imp_in[0] + imp_in[1] + imp_in[2]

    settle()

    for dx in (1, 3, 2):
        for g in range(3):
            gx[g, dx].wait_recv()
        forward_core(0, dx)
    for dx in (1, 3, 2):
        gx[3, dx].wait_recv()

    wrapped = lax.broadcasted_iota(jnp.int32, (B, D), 0) < shift

    def emit(half):
        for tl in range(NX):
            t = NX * half + tl
            for h in range(H):
                straight = gathered[t, 0:B, h, :]
                beyond = gathered[t, B : 2 * B, h, :]
                out_ref[t, :, h * D : (h + 1) * D] = jnp.where(wrapped, beyond, straight).astype(BF16)

    emit(mc)
    for copy in gc + list(ge.values()):
        copy.wait_recv()
    emit(other)

    settle()


def store(attended, importance, attended_out, importance_out, sem):
    copies = [
        pltpu.make_async_copy(attended, attended_out, sem.at[0]),
        pltpu.make_async_copy(importance, importance_out, sem.at[1]),
    ]
    for copy in copies:
        copy.start()
    for copy in copies:
        copy.wait()


def on_device(queries, cache_keys, stored_values, new_keys, decoded_values, keep_mask):
    any_space = pl.BlockSpec(memory_space=pl.ANY)
    vmem = pl.BlockSpec(memory_space=pltpu.VMEM)
    dma = pltpu.SemaphoreType.DMA
    attended, importance = pl.pallas_call(
        kernel,
        out_shape=(pltpu.VMEM((T, B, H * D), BF16), pltpu.VMEM((B // NY, S), F32)),
        in_specs=[any_space] * 6,
        out_specs=(vmem, vmem),
        scratch_shapes=[
            pltpu.VMEM((T, B, H, D), BF16),
            pltpu.VMEM((B, KV, S, D), BF16),
            pltpu.VMEM((B, KV, S, D), BF16),
            pltpu.VMEM((T, 2, KV, D), BF16),
            pltpu.VMEM((T, 2, KV, D), BF16),
            pltpu.VMEM((B, S), jnp.int32),
            pltpu.VMEM((B, T, H, D), F32),
            pltpu.VMEM((B, T, H, S), F32),
            pltpu.VMEM((H, D), F32),
            pltpu.VMEM((B, NX, H, D), F32),
            pltpu.VMEM((len(PEERS) - 1, FAR_ROWS, H, D), F32),
            pltpu.VMEM((NX, B, H, D), F32),
            pltpu.VMEM((NX - 1, B, H, D), F32),
            pltpu.VMEM((NZ, 2, H, D), F32),
            pltpu.VMEM((NZ - 1, 2, H, D), F32),
            pltpu.VMEM((T, 2 * B, H, D), F32),
            pltpu.VMEM((NY, B // NY, S), F32),
            pltpu.VMEM((NY - 1, B // NY, S), F32),
            pltpu.VMEM((2, NX, B, H, D), F32),
            pltpu.VMEM((len(PEERS), FAR_ROWS, H, D), F32),
            pltpu.VMEM((NX, B, H, D), F32),
            pltpu.VMEM((2, H, D), F32),
            pltpu.VMEM((len(PEERS) - 1, H, D), F32),
            pltpu.VMEM((H, D), F32),
            pltpu.VMEM((NZ - 1, H, D), F32),
            pltpu.VMEM((2, H, D), F32),
            dma((3,)),
            dma((3, NZ)),
            dma, dma, dma((len(PEERS) - 1,)), dma((len(PEERS) - 1,)),
            dma((len(PEERS) - 1,)), dma((len(PEERS) - 1,)), dma((3, NX - 1)), dma((3, NX - 1)),
            dma((NZ - 1,)), dma((NZ - 1,)), dma((NZ - 1,)), dma((NZ - 1,)),
            dma((NY - 1,)), dma((NY - 1,)),
            dma((NZ - 1,)), dma((NZ - 1,)), dma((4, NX - 1)), dma((4, NX - 1)),
            dma((NX - 1,)), dma((NX - 1,)), dma((2, NX)), dma((2, NX)),
            dma, dma,
            pltpu.SemaphoreType.REGULAR,
        ],
        compiler_params=pltpu.CompilerParams(
            collective_id=0, has_side_effects=True, vmem_limit_bytes=63 << 20
        ),
    )(queries, cache_keys, stored_values, new_keys, decoded_values, keep_mask)
    return pl.pallas_call(
        store,
        out_shape=(
            jax.ShapeDtypeStruct((T, B, H * D), BF16),
            jax.ShapeDtypeStruct((B // NY, S), F32),
        ),
        in_specs=[vmem, vmem],
        out_specs=(any_space, any_space),
        scratch_shapes=[dma((2,))],
    )(
        pltpu.with_memory_space_constraint(attended, pltpu.MemorySpace.VMEM),
        pltpu.with_memory_space_constraint(importance, pltpu.MemorySpace.VMEM),
    )


def solution(mesh):
    finer = Mesh(
        mesh.devices.reshape(mesh.shape["head"], NX, NZ, NC), ("head", "seq_0", "seq_1", "seq_2")
    )
    seq = ("seq_0", "seq_1", "seq_2")
    in_specs = (
        P(None, None, "head", None),
        P(None, "head", seq, None),
        P(None, "head", seq, None),
        P(None, None, "head", None),
        P(None, None, "head", None),
        P(None, seq),
    )
    out_specs = (P(None, None, "head"), P("head", seq))
    return jax.shard_map(
        on_device, mesh=finer, in_specs=in_specs, out_specs=out_specs, check_vma=False
    )
```

```python
import jax
import jax.numpy as jnp
from jax import lax
from jax.experimental import pallas as pl
from jax.experimental.pallas import tpu as pltpu
from jax.sharding import Mesh
from jax.sharding import PartitionSpec as P

F32 = jnp.float32
BF16 = jnp.bfloat16
MESH = pl.DeviceIdType.MESH
SCALE = 1.0 / 12.0
FAR_BELOW = -1e30

T, B, H, D = 8, 16, 8, 128
KV = 4
S = 128
NY, NX, NZ, NC = 4, 4, 8, 2
FAR_FIRST = (4, 3, 5, 2, 6, 1, 7)
OUT = FAR_FIRST + (0,)
SLOT = [(d + 2) % NZ for d in range(NZ)]
ROWS = [(2 * m + i, d, 2 * SLOT[d] + i) for m, d in enumerate(OUT) for i in range(2)]
FAR_ROWS = 2 * 3
NEAR_GROUPS = ((3, 2), (5, 2), (7, 1))
PEERS = [(dc, dx) for dc in range(NC) for dx in range(NX)]
SIBLING = PEERS.index((1, 0))
PEER_ORDER = (2, 6, 1, 3, 5, 7, 4)
FAR, NEAR = (5, 3), (0, 5)
BACK_GROUPS = ((2, 1, ()), (3, 2, (7, 6)), (0, 2, (1, 2)), (5, 3, (3, 5, 4)))
HEADS_ALL = 32
CONTEXT = S * NX * NZ * NC


def lane_of(tile, lane):
    return jnp.broadcast_to(tile[:, lane : lane + 1], (H, D))


def to_front(tile, lane):
    return pltpu.roll(tile, lax.rem(128 - lane, 128), 1)


def expand_heads(rows):
    sub = lax.broadcasted_iota(jnp.int32, (H, D), 0)
    out = jnp.broadcast_to(rows[KV - 1 : KV], (H, D))
    for k in range(KV - 2, -1, -1):
        out = jnp.where(sub < 2 * (k + 1), jnp.broadcast_to(rows[k : k + 1], (H, D)), out)
    return out


def kernel(
    q_hbm, k_hbm, v_hbm, nk_hbm, nv_hbm, mask_hbm,
    out_ref, imp_ref,
    q_ref, k_ref, v_ref, nk_ref, nv_ref, mask_ref,
    sums, exps, peaks, core_in, far_in, pair, x_in, z_out, z_in, gathered, imp_part, imp_in,
    f_pair, f_far, f_x, stat_own, stat_x, stat_group, stat_z, stat_full,
    in_sem, chunk_sem,
    cd_s, cd_r, xs_s, xs_r, xf_s, xf_r, xd_s, xd_r, zs_s, zs_r, zd_s, zd_r, y_s, y_r,
    gz_s, gz_r, gx_s, gx_r, ge_s, ge_r, gc_s, gc_r, hs_s, hs_r, ready,
):
    my = lax.axis_index("head")
    mx = lax.axis_index("seq_0")
    mz = lax.axis_index("seq_1")
    mc = lax.axis_index("seq_2")
    other = 1 - mc
    t_half = NX * mc
    t_own = t_half + mx
    base = lax.rem(mz + NZ - 2, NZ)

    def core_dev():
        return {"seq_2": other}

    def peer_core(p):
        return other if PEERS[p][0] else mc

    def peer_dev(p):
        return {"seq_0": lax.rem(mx + PEERS[p][1], NX), "seq_2": peer_core(p)}

    def x_dev(d):
        return {"seq_0": lax.rem(mx + d, NX)}

    def z_dev(d):
        return {"seq_1": lax.rem(mz + d, NZ)}

    def y_dev(d):
        return {"head": lax.rem(my + d, NY)}

    started = []

    def remote(src, dst, ss, rs, dev):
        copy = pltpu.make_async_remote_copy(
            src_ref=src, dst_ref=dst, send_sem=ss, recv_sem=rs, device_id=dev, device_id_type=MESH
        )
        copy.start()
        started.append(copy)
        return copy

    def settle():
        for copy in started:
            copy.wait_send()
        started.clear()

    barrier = pltpu.get_barrier_semaphore()
    partners = (
        [z_dev(d) for d in (2, 6, 1, 7)]
        + [peer_dev(p) for p in PEER_ORDER[:-1]]
        + [y_dev(d) for d in (2, 1, 3)]
        + [core_dev()]
    )
    for dev in partners:
        pl.semaphore_signal(barrier, inc=1, device_id=dev, device_id_type=MESH)

    def chunk_loads(m):
        rows = pl.ds(2 * lax.rem(mz + OUT[m], NZ), 2)
        mine = pl.ds(2 * m, 2)
        return [
            pltpu.make_async_copy(q_hbm.at[:, rows], q_ref.at[:, mine], chunk_sem.at[0, m]),
            pltpu.make_async_copy(k_hbm.at[rows], k_ref.at[mine], chunk_sem.at[1, m]),
            pltpu.make_async_copy(v_hbm.at[rows], v_ref.at[mine], chunk_sem.at[2, m]),
        ]

    def batch_row(d, i):
        return 2 * lax.rem(mz + d, NZ) + i

    b_own = 2 * mz
    small = [
        pltpu.make_async_copy(mask_hbm, mask_ref, in_sem.at[0]),
        pltpu.make_async_copy(nk_hbm.at[:, pl.ds(b_own, 2)], nk_ref, in_sem.at[1]),
        pltpu.make_async_copy(nv_hbm.at[:, pl.ds(b_own, 2)], nv_ref, in_sem.at[2]),
    ]
    small[0].start()
    loads = [chunk_loads(m) for m in range(NZ)]
    for copies in loads:
        for copy in copies:
            copy.start()
    for copy in small[1:]:
        copy.start()
    small[0].wait()

    lane = lax.broadcasted_iota(jnp.int32, (H, D), 1)
    row_kv = lax.rem(lax.broadcasted_iota(jnp.int32, (T * H, S), 0), H) // 2

    zero = jnp.zeros((H, D), F32)
    block_peak, block_total = zero, zero
    for batch in (range(0, 4), range(4, 8)):
        for m in batch:
            for copy in loads[m]:
                copy.wait()
        rows = ROWS[2 * batch[0] : 2 * batch[-1] + 2]
        scores = []
        for r, _, _ in rows:
            q = q_ref[:, r].astype(F32).reshape(T * H, D).astype(BF16)
            wide = lax.dot_general(
                q, k_ref[r].reshape(KV * S, D), (((1,), (1,)), ((), ())), preferred_element_type=F32
            )
            s = wide[:, (KV - 1) * S :]
            for k in range(KV - 2, -1, -1):
                s = jnp.where(row_kv == k, wide[:, k * S : (k + 1) * S], s)
            scores.append(s * SCALE)
        weights = []
        for (r, d, at), s in zip(rows, scores):
            b = batch_row(d, r % 2)
            keep = jnp.broadcast_to(mask_ref[pl.ds(b, 1), :], (T * H, S)) > 0
            m = jnp.max(jnp.where(keep, s, FAR_BELOW), axis=1, keepdims=True)
            e = jnp.where(keep, jnp.exp(s - m), 0.0)
            total = jnp.sum(e, axis=1, keepdims=True)
            exps[r] = e.reshape(T, H, S)
            weights.append(e)
            for t in range(T):
                here = lane == t * B + at
                part = slice(t * H, (t + 1) * H)
                block_peak = jnp.where(here, jnp.broadcast_to(m[part], (H, D)), block_peak)
                block_total = jnp.where(here, jnp.broadcast_to(total[part], (H, D)), block_total)
        for (r, _, _), e in zip(rows, weights):
            wide = jnp.concatenate(
                [jnp.where(row_kv == k, e, 0.0).astype(BF16) for k in range(KV)], axis=1
            )
            o = jnp.dot(wide, v_ref[r].reshape(KV * S, D), preferred_element_type=F32)
            sums[r] = o.reshape(T, H, D)
    peaks[...] = block_peak

    peak_tile, total_tile = block_peak, block_total
    for copy in small[1:]:
        copy.wait()
    for i in range(2):
        r = 2 * OUT.index(0) + i
        here = lane == t_own * B + 2 * SLOT[0] + i
        q = q_ref[t_own, r].astype(F32)
        ns = []
        for j in range(T):
            prod = q * expand_heads(nk_ref[j, i].astype(F32))
            sj = jnp.broadcast_to(jnp.sum(prod, axis=1, keepdims=True), (H, D)) * SCALE
            ns.append(jnp.where(j <= t_own, sj, FAR_BELOW))
        new_peak = ns[0]
        for j in range(1, T):
            new_peak = jnp.maximum(new_peak, ns[j])
        new_total, new_sum = zero, zero
        for j in range(T):
            ej = jnp.where(j <= t_own, jnp.exp(ns[j] - new_peak), 0.0)
            new_total = new_total + ej
            new_sum = new_sum + ej.astype(BF16).astype(F32) * expand_heads(nv_ref[j, i].astype(F32))
        old_peak = jnp.max(jnp.where(here, block_peak, -3e38), axis=1, keepdims=True)
        old_total = jnp.sum(jnp.where(here, block_total, 0.0), axis=1, keepdims=True)
        old_peak = jnp.broadcast_to(old_peak, (H, D))
        old_total = jnp.broadcast_to(old_total, (H, D))
        both = jnp.maximum(old_peak, new_peak)
        f_old = jnp.exp(old_peak - both)
        f_new = jnp.exp(new_peak - both)
        sums[r, t_own] = sums[r, t_own] * f_old + new_sum * f_new
        peak_tile = jnp.where(here, both, peak_tile)
        total_tile = jnp.where(here, old_total * f_old + new_total * f_new, total_tile)
    low = lane < D // 2

    def swap(tile):
        return pltpu.roll(tile, D // 2, 1)

    stat_own[0] = jnp.where(low, peak_tile, swap(total_tile))
    stat_own[1] = jnp.where(low, swap(peak_tile), total_tile)
    mine = stat_own[mc]

    pl.semaphore_wait(barrier, len(partners))
    for d in (2, 6):
        pl.semaphore_signal(ready, inc=1, device_id=z_dev(d), device_id_type=MESH)

    stats = [
        remote(stat_own.at[peer_core(p)], stat_x.at[p - 1], xs_s.at[p - 1], xs_r.at[p - 1], peer_dev(p))
        for p in PEER_ORDER
    ]
    far_rows = pl.ds(0, FAR_ROWS)
    far_copies = [
        remote(
            sums.at[far_rows, NX * peer_core(p) + lax.rem(mx + PEERS[p][1], NX)],
            far_in.at[p - 1], xf_s.at[p - 1], xf_r.at[p - 1], peer_dev(p),
        )
        for p in PEER_ORDER
    ]

    near_rows = pl.ds(FAR_ROWS, B - FAR_ROWS)
    core_copy = remote(
        sums.at[near_rows, pl.ds(NX * other, NX)], core_in.at[near_rows], cd_s, cd_r, core_dev()
    )
    stats[PEER_ORDER.index(SIBLING)].wait_recv()
    peak_c = stat_x[SIBLING - 1]
    pair_peak = jnp.maximum(mine, peak_c)
    fo = jnp.exp(mine - pair_peak)
    fc = jnp.exp(peak_c - pair_peak)
    for r, _, at in ROWS[FAR_ROWS:]:
        for tl in range(NX):
            f_pair[0, tl, r] = lane_of(fo, tl * B + at)
            f_pair[1, tl, r] = lane_of(fc, tl * B + at)

    core_copy.wait_recv()
    x_copies = []
    for g, (first, count) in enumerate(NEAR_GROUPS):
        for tl in range(NX):
            for r in range(2 * first, 2 * (first + count)):
                pair[tl, r] = (
                    sums[r, t_half + tl] * f_pair[0, tl, r] + core_in[r, tl] * f_pair[1, tl, r]
                )
        rows = pl.ds(2 * first, 2 * count)
        x_copies.append(
            [
                remote(
                    pair.at[lax.rem(mx + d, NX), rows], x_in.at[d - 1, rows],
                    xd_s.at[g, d - 1], xd_r.at[g, d - 1], x_dev(d),
                )
                for d in (2, 1, 3)
            ]
        )
    for p, copy in zip(PEER_ORDER, stats):
        if p != SIBLING:
            copy.wait_recv()
    peer_peak = [mine] + [stat_x[p - 1] for p in range(1, len(PEERS))]
    group_peak = mine
    for p in range(1, len(PEERS)):
        group_peak = jnp.maximum(group_peak, peer_peak[p])
    factors = [jnp.exp(one - group_peak) for one in peer_peak]
    group_total = swap(mine) * factors[0]
    for p in range(1, len(PEERS)):
        group_total = group_total + swap(peer_peak[p]) * factors[p]

    shift = 2 * base
    in_row = lax.rem(lane, B)

    def by_row(tile):
        return jnp.where(
            in_row >= shift, pltpu.roll(tile, shift, 1), pltpu.roll(tile, lax.rem(shift + 112, 128), 1)
        )

    def by_slot(tile):
        return jnp.where(
            in_row < B - shift,
            pltpu.roll(tile, lax.rem(128 - shift, 128), 1),
            pltpu.roll(tile, lax.rem(144 - shift, 128), 1),
        )

    group_peak = by_row(group_peak)
    group_total = by_row(group_total)
    stat_group[...] = jnp.where(low, group_peak, swap(group_total))
    pl.semaphore_wait(ready, 2)
    z_stats = [
        remote(stat_group, stat_z.at[d - 1], zs_s.at[d - 1], zs_r.at[d - 1], z_dev(d))
        for d in FAR_FIRST
    ]
    for p in range(len(PEERS)):
        f = to_front(factors[p], mx * B)
        for r, _, at in ROWS[:FAR_ROWS]:
            f_far[p, r] = lane_of(f, at)
    for dx in range(NX):
        f = to_front(jnp.maximum(factors[dx], factors[NX + dx]), mx * B)
        for r, _, at in ROWS[FAR_ROWS:]:
            f_x[dx, r] = lane_of(f, at)
    z_copies = []

    def send_z(m):
        d = OUT[m]
        if d > 0:
            z_copies.append(
                remote(z_out.at[m], z_in.at[d - 1], zd_s.at[d - 1], zd_r.at[d - 1], z_dev(d))
            )

    for copy in far_copies:
        copy.wait_recv()
    for m in range(FAR_ROWS // 2):
        for i in range(2):
            r = 2 * m + i
            acc = sums[r, t_own] * f_far[0, r]
            for p in range(1, len(PEERS)):
                acc = acc + far_in[p - 1, r] * f_far[p, r]
            z_out[m, i] = acc
        send_z(m)
    for g, (first, count) in enumerate(NEAR_GROUPS):
        for copy in x_copies[g]:
            copy.wait_recv()
        for m in range(first, first + count):
            for i in range(2):
                r = 2 * m + i
                acc = pair[mx, r] * f_x[0, r]
                for dx in range(1, NX):
                    acc = acc + x_in[dx - 1, r] * f_x[dx, r]
                z_out[m, i] = acc
            send_z(m)
    for copy in z_stats:
        copy.wait_recv()
    peak = group_peak
    for d in range(1, NZ):
        peak = jnp.maximum(peak, stat_z[d - 1])
    factors = [jnp.exp(group_peak - peak)]
    total = group_total * factors[0]
    for d in range(1, NZ):
        f = jnp.exp(stat_z[d - 1] - peak)
        factors.append(f)
        total = total + swap(stat_z[d - 1]) * f
    inverse = 1.0 / total
    front = [to_front(f * inverse, mx * B + b_own) for f in factors]
    scale = [[lane_of(f, i) for f in front] for i in range(2)]
    stat_full[mc] = jnp.where(low, peak, swap(total))
    half_stat = remote(stat_full.at[mc], stat_full.at[mc], hs_s, hs_r, core_dev())
    for copy in z_copies:
        copy.wait_recv()
    for i in range(2):
        acc = z_out[OUT.index(0), i] * scale[i][0]
        for d in range(1, NZ):
            acc = acc + z_in[d - 1, i] * scale[i][d]
        gathered[t_own, 2 * (base + SLOT[0]) + i] = acc

    own = gathered.at[t_own, pl.ds(2 * (base + SLOT[0]), 2)]
    gz = {}
    for d in FAR_FIRST:
        place = lax.rem(mz + d + NZ - 2, NZ) + SLOT[NZ - d]
        gz[d] = remote(
            own, gathered.at[t_own, pl.ds(2 * place, 2)], gz_s.at[d - 1], gz_r.at[d - 1], z_dev(d)
        )

    gx, ge, gc = {}, {}, []

    def span_of(t, first, count):
        return gathered.at[t, pl.ds(2 * (base + first), 2 * count)]

    def forward_x(g):
        first, count, arrivals = BACK_GROUPS[g]
        for d in arrivals:
            gz[d].wait_recv()
        span = span_of(t_own, first, count)
        for dx in (2, 1, 3):
            gx[g, dx] = remote(span, span, gx_s.at[g, dx - 1], gx_r.at[g, dx - 1], x_dev(dx))
            if g == 3:
                ge[dx] = remote(
                    span, span, ge_s.at[dx - 1], ge_r.at[dx - 1], peer_dev(NX + dx)
                )

    def forward_core(g, dx):
        span = span_of(t_half + lax.rem(mx + NX - dx, NX), *(NEAR, FAR)[g])
        gc.append(remote(span, span, gc_s.at[g, dx], gc_r.at[g, dx], core_dev()))

    forward_x(0)

    half_stat.wait_recv()
    full_peak = by_slot(jnp.where(low, stat_full[0], swap(stat_full[1])))
    full_total = by_slot(jnp.where(low, swap(stat_full[0]), stat_full[1]))
    share = jnp.exp(peaks[...] - full_peak) / full_total * (CONTEXT / (T * HEADS_ALL))
    for r, d, at in ROWS:
        acc = exps[r, 0] * lane_of(share, at)
        for t in range(1, T):
            acc = acc + exps[r, t] * lane_of(share, t * B + at)
        b = batch_row(d, r % 2)
        imp_part[b // 4, pl.ds(lax.rem(b, 4), 1)] = jnp.sum(acc, axis=0, keepdims=True)
    y_copies = []
    for d in (2, 1, 3):
        y_copies.append(
            remote(
                imp_part.at[lax.rem(my + d, NY)], imp_in.at[d - 1], y_s.at[d - 1], y_r.at[d - 1],
                y_dev(d),
            )
        )

    settle()

    forward_x(1)
    forward_x(2)
    forward_core(0, 0)
    forward_x(3)
    forward_core(1, 0)

    for copy in y_copies:
        copy.wait_recv()
    imp_ref[...] = imp_part[my] + imp_in[0] + imp_in[1] + imp_in[2]

    settle()

    for dx in (1, 3, 2):
        for g in range(3):
            gx[g, dx].wait_recv()
        forward_core(0, dx)
    for dx in (1, 3, 2):
        gx[3, dx].wait_recv()

    wrapped = lax.broadcasted_iota(jnp.int32, (B, D), 0) < shift

    def emit(half):
        for tl in range(NX):
            t = NX * half + tl
            for h in range(H):
                straight = gathered[t, 0:B, h, :]
                beyond = gathered[t, B : 2 * B, h, :]
                out_ref[t, :, h * D : (h + 1) * D] = jnp.where(wrapped, beyond, straight).astype(BF16)

    emit(mc)
    for copy in gc + list(ge.values()):
        copy.wait_recv()
    emit(other)

    settle()


def store(attended, importance, attended_out, importance_out, sem):
    copies = [
        pltpu.make_async_copy(attended.at[pl.ds(2 * i, 2)], attended_out.at[pl.ds(2 * i, 2)], sem.at[i])
        for i in range(T // 2)
    ] + [pltpu.make_async_copy(importance, importance_out, sem.at[T // 2])]
    for copy in copies:
        copy.start()
    for copy in copies:
        copy.wait()


def on_device(queries, cache_keys, stored_values, new_keys, decoded_values, keep_mask):
    any_space = pl.BlockSpec(memory_space=pl.ANY)
    vmem = pl.BlockSpec(memory_space=pltpu.VMEM)
    dma = pltpu.SemaphoreType.DMA
    attended, importance = pl.pallas_call(
        kernel,
        out_shape=(pltpu.VMEM((T, B, H * D), BF16), pltpu.VMEM((B // NY, S), F32)),
        in_specs=[any_space] * 6,
        out_specs=(vmem, vmem),
        scratch_shapes=[
            pltpu.VMEM((T, B, H, D), BF16),
            pltpu.VMEM((B, KV, S, D), BF16),
            pltpu.VMEM((B, KV, S, D), BF16),
            pltpu.VMEM((T, 2, KV, D), BF16),
            pltpu.VMEM((T, 2, KV, D), BF16),
            pltpu.VMEM((B, S), jnp.int32),
            pltpu.VMEM((B, T, H, D), F32),
            pltpu.VMEM((B, T, H, S), F32),
            pltpu.VMEM((H, D), F32),
            pltpu.VMEM((B, NX, H, D), F32),
            pltpu.VMEM((len(PEERS) - 1, FAR_ROWS, H, D), F32),
            pltpu.VMEM((NX, B, H, D), F32),
            pltpu.VMEM((NX - 1, B, H, D), F32),
            pltpu.VMEM((NZ, 2, H, D), F32),
            pltpu.VMEM((NZ - 1, 2, H, D), F32),
            pltpu.VMEM((T, 2 * B, H, D), F32),
            pltpu.VMEM((NY, B // NY, S), F32),
            pltpu.VMEM((NY - 1, B // NY, S), F32),
            pltpu.VMEM((2, NX, B, H, D), F32),
            pltpu.VMEM((len(PEERS), FAR_ROWS, H, D), F32),
            pltpu.VMEM((NX, B, H, D), F32),
            pltpu.VMEM((2, H, D), F32),
            pltpu.VMEM((len(PEERS) - 1, H, D), F32),
            pltpu.VMEM((H, D), F32),
            pltpu.VMEM((NZ - 1, H, D), F32),
            pltpu.VMEM((2, H, D), F32),
            dma((3,)),
            dma((3, NZ)),
            dma, dma, dma((len(PEERS) - 1,)), dma((len(PEERS) - 1,)),
            dma((len(PEERS) - 1,)), dma((len(PEERS) - 1,)), dma((3, NX - 1)), dma((3, NX - 1)),
            dma((NZ - 1,)), dma((NZ - 1,)), dma((NZ - 1,)), dma((NZ - 1,)),
            dma((NY - 1,)), dma((NY - 1,)),
            dma((NZ - 1,)), dma((NZ - 1,)), dma((4, NX - 1)), dma((4, NX - 1)),
            dma((NX - 1,)), dma((NX - 1,)), dma((2, NX)), dma((2, NX)),
            dma, dma,
            pltpu.SemaphoreType.REGULAR,
        ],
        compiler_params=pltpu.CompilerParams(
            collective_id=0, has_side_effects=True, vmem_limit_bytes=63 << 20
        ),
    )(queries, cache_keys, stored_values, new_keys, decoded_values, keep_mask)
    return pl.pallas_call(
        store,
        out_shape=(
            jax.ShapeDtypeStruct((T, B, H * D), BF16),
            jax.ShapeDtypeStruct((B // NY, S), F32),
        ),
        in_specs=[vmem, vmem],
        out_specs=(any_space, any_space),
        scratch_shapes=[dma((T // 2 + 1,))],
    )(
        pltpu.with_memory_space_constraint(attended, pltpu.MemorySpace.VMEM),
        pltpu.with_memory_space_constraint(importance, pltpu.MemorySpace.VMEM),
    )


def solution(mesh):
    finer = Mesh(
        mesh.devices.reshape(mesh.shape["head"], NX, NZ, NC), ("head", "seq_0", "seq_1", "seq_2")
    )
    seq = ("seq_0", "seq_1", "seq_2")
    in_specs = (
        P(None, None, "head", None),
        P(None, "head", seq, None),
        P(None, "head", seq, None),
        P(None, None, "head", None),
        P(None, None, "head", None),
        P(None, seq),
    )
    out_specs = (P(None, None, "head"), P("head", seq))
    return jax.shard_map(
        on_device, mesh=finer, in_specs=in_specs, out_specs=out_specs, check_vma=False
    )
```
